32 devices in a mesh: seqmaj: 4 (over y, x), seqmin: 8 (over z, core).
Axes of the slice: x: 2, y: 2, z: 4, core: 2. Of those that a mesh axis runs over, the one named last changes fastest.
Arguments:
- q_first: bfloat16 [4096, 2048], P(('seqmaj', 'seqmin')), may hold values from -6 to 6
- k_first: bfloat16 [4096, 2048], P(('seqmaj', 'seqmin')), may hold values from -6 to 6
- v_first: bfloat16 [4096, 2048], P(('seqmaj', 'seqmin')), may hold values from -6 to 6
- mr_filter: bfloat16 [128, 2048], replicated, may hold values from -0.5 to 0.5
- mr_skip: float32 [2048], replicated, may hold values from -4 to 4
- value_weight: bfloat16 [2048, 2048], replicated, may hold values from -0.125 to 0.125
- q_second: bfloat16 [4096, 2048], P(('seqmaj', 'seqmin')), may hold values from -6 to 6
- k_second: bfloat16 [4096, 2048], P(('seqmaj', 'seqmin')), may hold values from -6 to 6
- li_residue: float32 [16, 2048], replicated, may hold values from -3 to 3
- li_rate: float32 [16, 2048], replicated, may hold values from 0.00012207031 to 0.033333335
- li_skip: float32 [2048], replicated, may hold values from -4 to 4
- out_second: bfloat16 [2048, 2048], replicated, may hold values from -0.0625 to 0.0625
Outputs:
- mixed: bfloat16 [4096, 2048], P(('seqmaj', 'seqmin'))
The draws below stay inside these ranges and needn't reach their ends.
All inputs are finite; a program needn't handle non-finite values.
Results may differ from the reference program's by a relative error of at most 0.015.
Values may be sent and summed in bfloat16 or wider, within the bound.
A program may use at most 128 MiB of HBM per device.

```python
import math
import jax
import jax.numpy as jnp
from jax import lax

C = 2048
MR_TAPS = 128
MODES = 16
TOKENS = 4096


def block_scale(stream_key, dims, pieces, low, top_value):
    factor_of, own = 1.0, jax.random.fold_in(stream_key, 6)
    for dim, blocks in pieces:
        steps = jnp.exp(jax.random.uniform(jax.random.fold_in(own, dim), (blocks,), jnp.float32, low / len(pieces), top_value / len(pieces)))
        factor_of = factor_of * jnp.repeat(steps, dims[dim] // blocks).reshape([-1 if axis == dim else 1 for axis in range(len(dims))])
    return factor_of


def scatter_about(stream_key, shape, scale, reach, split=(), dtype=jnp.bfloat16):
    drawn = scale * jax.random.normal(stream_key, shape, jnp.float32)
    if split:
        drawn = drawn * block_scale(stream_key, shape, split, -0.22, 0.18)
    return jnp.clip(drawn, -reach, reach).astype(dtype)


def setup_inputs(seed: int = 0) -> dict:
    key_of = jax.random.split(jax.random.key(seed), 13)
    return {
        "q_first": scatter_about(key_of[0], (TOKENS, C), 1.0, 6.0, ((0, 32),)),
        "k_first": scatter_about(key_of[1], (TOKENS, C), 1.0, 6.0, ((0, 32),)),
        "v_first": scatter_about(key_of[2], (TOKENS, C), 1.0, 6.0, ((0, 32),)),
        "mr_filter": scatter_about(key_of[3], (MR_TAPS, C), MR_TAPS ** -0.5, 0.5),
        "mr_skip": scatter_about(key_of[4], (C,), 1.0, 4.0, (), jnp.float32),
        "value_weight": scatter_about(key_of[5], (C, C), C ** -0.5, 0.125),
        "q_second": scatter_about(key_of[6], (TOKENS, C), 1.0, 6.0, ((0, 32),)),
        "k_second": scatter_about(key_of[7], (TOKENS, C), 1.0, 6.0, ((0, 32),)),
        "li_residue": scatter_about(key_of[8], (MODES, C), 0.5, 3.0, (), jnp.float32),
        "li_rate": jnp.clip(jnp.exp(jax.random.uniform(key_of[9], (MODES, C), jnp.float32, math.log(0.00012207031), math.log(0.033333335))), 0.00012207031, 0.033333335),
        "li_skip": scatter_about(key_of[10], (C,), 1.0, 4.0, (), jnp.float32),
        "out_second": scatter_about(key_of[11], (C, C), (4 * C) ** -0.5, 0.0625),
    }


def long_block(signal_block, residue_block, rate_block):
    times = jnp.arange(TOKENS).astype(jnp.float32)
    weight = residue_block * jnp.sqrt(rate_block)
    long_filter = lax.optimization_barrier(jnp.sum(weight[None, :, :] * jnp.exp(-rate_block[None, :, :] * times[:, None, None]), axis=1))
    padded_size = 2 * TOKENS
    product = jnp.fft.rfft(signal_block, n=padded_size, axis=0) * jnp.fft.rfft(long_filter, n=padded_size, axis=0)
    return jnp.fft.irfft(product, n=padded_size, axis=0)[:TOKENS]

def short_convolution(padded, taps):

    def add_tap(step, total):
        start = (MR_TAPS - 1 - step).astype(jnp.int32)
        piece = lax.dynamic_slice_in_dim(padded, start, TOKENS, 0)
        row = lax.dynamic_slice_in_dim(taps, step.astype(jnp.int32), 1, 0)
        return total + row * piece
    initial = jnp.zeros((TOKENS, C), jnp.float32)
    return lax.fori_loop(jnp.int32(0), jnp.int32(MR_TAPS), add_tap, initial)

def reference(q_first, k_first, v_first, mr_filter, mr_skip, value_weight, q_second, k_second, li_residue, li_rate, li_skip, out_second):
    gated_first = (k_first.astype(jnp.float32) * v_first.astype(jnp.float32)).astype(jnp.bfloat16)
    padded = jnp.concatenate([jnp.zeros((MR_TAPS - 1, C), jnp.float32), gated_first.astype(jnp.float32)], axis=0)
    short_conv = short_convolution(padded, mr_filter.astype(jnp.float32))
    first_act = (q_first.astype(jnp.float32) * (short_conv + mr_skip[None, :] * gated_first.astype(jnp.float32))).astype(jnp.bfloat16)
    v_second = jnp.dot(first_act, value_weight, preferred_element_type=jnp.float32).astype(jnp.bfloat16)
    gated_second = (k_second.astype(jnp.float32) * v_second.astype(jnp.float32)).astype(jnp.bfloat16)
    block_count = C // 16
    signal_blocks = jnp.moveaxis(gated_second.astype(jnp.float32).reshape(TOKENS, block_count, 16), 1, 0)
    residue_blocks = jnp.moveaxis(li_residue.reshape(MODES, block_count, 16), 1, 0)
    rate_blocks = jnp.moveaxis(li_rate.reshape(MODES, block_count, 16), 1, 0)
    conv_blocks = lax.map(lambda items: long_block(items[0], items[1], items[2]), (signal_blocks, residue_blocks, rate_blocks))
    long_conv = jnp.moveaxis(conv_blocks, 0, 1).reshape(TOKENS, C)
    second_act = (q_second.astype(jnp.float32) * (long_conv + li_skip[None, :] * gated_second.astype(jnp.float32))).astype(jnp.bfloat16)
    return jnp.dot(second_act, out_second, preferred_element_type=jnp.float32).astype(jnp.bfloat16)
```

```python
import functools

import jax
import jax.numpy as jnp
import ml_dtypes
import numpy as np
from jax import lax
from jax.experimental import pallas as pl
from jax.experimental.pallas import tpu as pltpu
from jax.sharding import PartitionSpec as P

axes = ("seqmaj", "seqmin")
MESH = pl.DeviceIdType.MESH
f32, bf16 = jnp.float32, jnp.bfloat16
WIDE = 512
LANES = 128
NODES = 16
OWNERS = 8


def split(table):
    high = table.astype(ml_dtypes.bfloat16).astype(np.float64)
    return high, table - high


def tables(rows):
    size = 2 * rows
    theta = 2.0 * np.pi * (np.arange(rows) + 0.5) / size
    angle = theta[:, None] * np.arange(size)[None, :]
    forward = np.concatenate([np.cos(angle), np.sin(angle)], axis=0)
    inverse = forward.T / rows
    nodes = 0.5 * (rows - 1) * (1.0 - np.cos(np.pi * (np.arange(NODES) + 0.5) / NODES))
    t = np.arange(rows, dtype=np.float64)
    basis = np.stack([
        np.prod([(t - nodes[m]) / (nodes[k] - nodes[m]) for m in range(NODES) if m != k], axis=0) for k in range(NODES)
    ], axis=1)
    high, low = split(basis)
    expand = np.concatenate([high, high, low], axis=1)
    moments = np.concatenate([high[::-1].T, low[::-1].T], axis=0)
    high, low = split(forward[:, :rows] @ basis)
    lift = np.concatenate([high, high, low], axis=1)
    at = np.broadcast_to(nodes[:, None], (NODES, LANES))
    return [jnp.asarray(a, bf16) for a in (forward, inverse, expand, moments, lift)] + [jnp.asarray(at, f32)], nodes


def mm(a, b):
    return jnp.dot(a, b, preferred_element_type=f32)


def spectral_product(x, h):
    half = x.shape[0] // 2
    xc, xs, hc, hs = x[:half], x[half:], h[:half], h[half:]
    return jnp.concatenate([xc * hc - xs * hs, xc * hs + xs * hc], axis=0).astype(bf16)


def stacked(x):
    high = x.astype(bf16)
    low = (x - high.astype(f32)).astype(bf16)
    return jnp.concatenate([high, low, high], axis=0)


def kernel(
    n, minor, nodes,
    q1h, k1h, v1h, tapsh, skip1h, w1h, q2h, k2h, resh, rateh, skip2h, w2h, fwdh, invh, expandh, momh, lifth, ath, out,
    q1, k1, v1, taps, skip1, w1, q2, k2, res, rate, skip2, w2, fwd, inv, expand, mom, lift, at,
    win, h1, h2, by_node, by_mode, coef, acc, y, g2, ends, got, sout, sin,
    in_sem, w1_sem, w2_sem, bsend, brecv, esend, erecv, ssend, srecv, ready,
):
    rows, channels = q1.shape
    modes = rate.shape[0]
    chunks = channels // WIDE
    owners = ends.shape[0]
    tiles = ends.shape[1] // modes
    me = lax.axis_index("seqmaj") * minor + lax.axis_index("seqmin")
    first = n - 2 * owners
    mine = lax.div(jnp.maximum(me - first, 0), 2)
    owner = jnp.logical_and(me >= first, lax.rem(me - first + n, 2) == 0)

    def place(d):
        return (lax.div(d, minor), lax.rem(d, minor))

    barrier = pltpu.get_barrier_semaphore()

    @pl.when(me > 0)
    def _():
        @pl.when(jnp.logical_or(me - 1 < first, lax.rem(me - 1 - first + n, 2) == 1))
        def _():
            pl.semaphore_signal(barrier, inc=1, device_id=place(me - 1), device_id_type=MESH)

    loads = {}
    for i, (name, src, dst) in enumerate([
        ("k1", k1h, k1), ("v1", v1h, v1), ("rate", rateh, rate), ("res", resh, res), ("at", ath, at), ("fwd", fwdh, fwd),
        ("taps", tapsh, taps), ("lift", lifth, lift), ("inv", invh, inv), ("q1", q1h, q1), ("skip1", skip1h, skip1),
        ("k2", k2h, k2), ("skip2", skip2h, skip2), ("q2", q2h, q2), ("mom", momh, mom), ("expand", expandh, expand),
    ]):
        loads[name] = pltpu.make_async_copy(src, dst, in_sem.at[i])
        loads[name].start()

    def weight_load(src, dst, sem, c):
        return pltpu.make_async_copy(src.at[pl.ds(c * WIDE, WIDE), :], dst.at[pl.ds(c * WIDE, WIDE), :], sem.at[c])

    for c in range(chunks):
        weight_load(w1h, w1, w1_sem, c).start()

    @pl.loop(0, owners)
    def _(j):
        @pl.when(first + 2 * j != me)
        def _():
            pl.semaphore_signal(barrier, inc=1, device_id=place(first + 2 * j), device_id_type=MESH)

    for c in range(chunks):
        weight_load(w2h, w2, w2_sem, c).start()

    def cols(c):
        return slice(c * WIDE, (c + 1) * WIDE)

    loads["k1"].wait()
    loads["v1"].wait()
    for c in range(chunks):
        win[c, rows:, :] = (k1[:, cols(c)].astype(f32) * v1[:, cols(c)].astype(f32)).astype(bf16)

    def border(c):
        return pltpu.make_async_remote_copy(
            src_ref=win.at[c, pl.ds(rows, rows), :], dst_ref=win.at[c, pl.ds(0, rows), :],
            send_sem=bsend.at[c], recv_sem=brecv.at[c],
            device_id=place(lax.rem(me + 1, n)), device_id_type=MESH,
        )

    def send_border():
        @pl.when(me < n - 1)
        def _():
            for c in range(chunks):
                border(c).start()

    @pl.when(jnp.logical_and(jnp.logical_not(owner), me < n - 1))
    def _():
        pl.semaphore_wait(barrier, 1)
        send_border()

    @pl.when(me == 0)
    def _():
        for c in range(chunks):
            win[c, :rows, :] = jnp.zeros((rows, WIDE), bf16)

    loads["rate"].wait()
    loads["res"].wait()
    loads["at"].wait()

    @pl.loop(0, channels // LANES)
    def _(b):
        lane = pl.ds(pl.multiple_of(b * LANES, LANES), LANES)
        lam = rate[:, lane]
        weight = res[:, lane] * jnp.sqrt(lam)
        for k in range(NODES):
            by_node[k, :, lane] = jnp.exp(lam * (-float(nodes[k])))
        total = jnp.zeros((NODES, LANES), f32)
        where = at[...]
        for r in range(modes):
            value = jnp.exp(-(jnp.broadcast_to(lam[r : r + 1], (NODES, LANES)) * where))
            by_mode[r, :, lane] = value
            total = total + value * jnp.broadcast_to(weight[r : r + 1], (NODES, LANES))
        coef[:, lane] = total

    loads["fwd"].wait()
    loads["taps"].wait()
    loads["lift"].wait()

    for c in range(chunks):
        h1[c] = mm(fwd[:, :rows], taps[:, cols(c)])
        h2[c] = mm(lift[...], stacked(coef[:, cols(c)]))

    @pl.when(owner)
    def _():
        pl.semaphore_wait(barrier, n - 1)
        send_border()

        @pl.loop(1, n)
        def _(p):
            pl.semaphore_signal(ready, inc=1, device_id=place(lax.rem(me + p, n)), device_id_type=MESH)

    loads["inv"].wait()
    loads["q1"].wait()
    loads["skip1"].wait()

    def first_act(c):
        @pl.when(me > 0)
        def _():
            border(c).wait_recv()

        spec = spectral_product(mm(fwd[...], win[c]), h1[c])
        short = mm(inv[rows:, :], spec)
        own = win[c, rows:, :].astype(f32)
        return (q1[:, cols(c)].astype(f32) * (short + skip1[:, cols(c)] * own)).astype(bf16)

    for c in range(chunks - 1):
        act = first_act(c)
        weight_load(w1h, w1, w1_sem, c).wait()
        if c == 0:
            acc[...] = mm(act, w1[cols(c), :])
        else:
            acc[...] += mm(act, w1[cols(c), :])

    last = chunks - 1
    act = first_act(last)
    weight_load(w1h, w1, w1_sem, last).wait()
    loads["k2"].wait()
    loads["mom"].wait()

    @pl.when(owner)
    def _():
        pl.semaphore_wait(ready, owners - 1)

    @pl.when(jnp.logical_not(owner))
    def _():
        pl.semaphore_wait(ready, owners)

    def ends_copy(j):
        return pltpu.make_async_remote_copy(
            src_ref=ends.at[j], dst_ref=got.at[me], send_sem=esend.at[0], recv_sem=erecv.at[me],
            device_id=place(first + 2 * j), device_id_type=MESH,
        )

    per_chunk = WIDE // LANES
    for c in range(chunks):
        v = acc[:, cols(c)] + mm(act, w1[cols(last), cols(c)])
        gated = (k2[:, cols(c)].astype(f32) * v.astype(bf16).astype(f32)).astype(bf16)
        g2[c] = gated
        moment = mm(mom[...], gated)
        moment = moment[:NODES] + moment[NODES:]
        e = jnp.zeros((modes, WIDE), f32)
        for k in range(NODES):
            e = e + by_node[k, :, cols(c)] * jnp.broadcast_to(moment[k : k + 1], (modes, WIDE))
        for i in range(per_chunk):
            o, s = divmod(c * per_chunk + i, tiles)
            ends[o, s * modes : (s + 1) * modes, :] = e[:, i * LANES : (i + 1) * LANES].astype(bf16)
            if s == tiles - 1:

                @pl.when(jnp.logical_and(me < n - 1, first + 2 * o != me))
                def _():
                    ends_copy(o).start()

    loads["skip2"].wait()
    for c in range(chunks):
        gated = g2[c]
        spec = spectral_product(mm(fwd[:, :rows], gated), h2[c])
        y[c] = mm(inv[:rows, :], spec) + skip2[:, cols(c)] * gated.astype(f32)

    def state_copy(d):
        return pltpu.make_async_remote_copy(
            src_ref=sout.at[d], dst_ref=sin.at[mine], send_sem=ssend.at[0], recv_sem=srecv.at[mine],
            device_id=place(d), device_id_type=MESH,
        )

    @pl.when(owner)
    def _():
        got[me] = ends[mine]
        decays, scales = [], []
        for s in range(tiles):
            lane = pl.ds(pl.multiple_of((mine * tiles + s) * LANES, LANES), LANES)
            lam = rate[:, lane]
            decays.append(jnp.exp(lam * (-float(rows))))
            scales.append(res[:, lane] * jnp.sqrt(lam) * jnp.exp(-lam))
        decay, scale = jnp.concatenate(decays, axis=0), jnp.concatenate(scales, axis=0)

        def serve(p, state):
            @pl.when(p != me)
            def _():
                pltpu.make_async_remote_copy(
                    src_ref=ends.at[0], dst_ref=got.at[p], send_sem=esend.at[0], recv_sem=erecv.at[p],
                    device_id=place(lax.rem(me + 1, n)), device_id_type=MESH,
                ).wait_recv()

            state = state * decay + got[p].astype(f32)
            sout[p + 1] = (state * scale).astype(bf16)

            @pl.when(p + 1 != me)
            def _():
                state_copy(p + 1).start()

            @pl.when(p + 1 == me)
            def _():
                sin[mine] = sout[me]

            return state

        lax.fori_loop(0, n - 1, serve, jnp.zeros((tiles * modes, LANES), f32))

    loads["q2"].wait()
    loads["expand"].wait()

    @pl.when(me == 0)
    def _():
        sin[...] = jnp.zeros_like(sin)

    def second_act(c):
        from_states = []
        for i in range(per_chunk):
            o, s = divmod(c * per_chunk + i, tiles)
            if s == 0:

                @pl.when(jnp.logical_and(me > 0, first + 2 * o != me))
                def _():
                    pltpu.make_async_remote_copy(
                        src_ref=sout.at[0], dst_ref=sin.at[o], send_sem=ssend.at[0], recv_sem=srecv.at[o],
                        device_id=place(lax.rem(me + 1, n)), device_id_type=MESH,
                    ).wait_recv()

            from_states.append(sin[o, s * modes : (s + 1) * modes, :].astype(f32))
        state = jnp.concatenate(from_states, axis=1)
        total = jnp.zeros((NODES, WIDE), f32)
        for r in range(modes):
            total = total + by_mode[r, :, cols(c)] * jnp.broadcast_to(state[r : r + 1], (NODES, WIDE))
        return (q2[:, cols(c)].astype(f32) * (y[c] + mm(expand[...], stacked(total)))).astype(bf16)

    for c in range(chunks):
        act = second_act(c)
        weight_load(w2h, w2, w2_sem, c).wait()
        if c == 0:
            acc[...] = mm(act, w2[cols(c), :])
        elif c < last:
            acc[...] += mm(act, w2[cols(c), :])
        else:
            out[...] = (acc[...] + mm(act, w2[cols(c), :])).astype(bf16)

    @pl.when(me < n - 1)
    def _():
        for c in range(chunks):
            border(c).wait_send()

    def sent(src, dst, count, send_sem, recv_sem):
        span = pl.ds(0, count)
        pltpu.make_async_remote_copy(
            src_ref=src.at[span], dst_ref=dst.at[span], send_sem=send_sem.at[0], recv_sem=recv_sem.at[0],
            device_id=place(lax.rem(me + 1, n)), device_id_type=MESH,
        ).wait_send()

    @pl.when(jnp.logical_and(me < n - 1, jnp.logical_not(owner)))
    def _():
        sent(ends, got, owners, esend, erecv)

    @pl.when(jnp.logical_and(me < n - 1, owner))
    def _():
        sent(ends, got, owners - 1, esend, erecv)

    @pl.when(owner)
    def _():
        @pl.when(me > 0)
        def _():
            sent(sout, got, n - 2, ssend, srecv)

        @pl.when(me == 0)
        def _():
            sent(sout, got, n - 1, ssend, srecv)


def local(q1, k1, v1, taps, skip1, w1, q2, k2, residue, rate, skip2, w2):
    rows, channels = q1.shape
    modes = rate.shape[0]
    minor = lax.axis_size("seqmin")
    n = lax.axis_size("seqmaj") * minor
    constants, nodes = tables(rows)
    operands = (q1, k1, v1, taps, skip1[None], w1, q2, k2, residue, rate, skip2[None], w2, *constants)
    chunks, tiles = channels // WIDE, channels // (LANES * OWNERS)
    scratch = [pltpu.VMEM(a.shape, a.dtype) for a in operands] + [
        pltpu.VMEM((chunks, 2 * rows, WIDE), bf16),
        pltpu.VMEM((chunks, 2 * rows, WIDE), f32),
        pltpu.VMEM((chunks, 2 * rows, WIDE), f32),
        pltpu.VMEM((NODES, modes, channels), f32),
        pltpu.VMEM((modes, NODES, channels), f32),
        pltpu.VMEM((NODES, channels), f32),
        pltpu.VMEM((rows, channels), f32),
        pltpu.VMEM((chunks, rows, WIDE), f32),
        pltpu.VMEM((chunks, rows, WIDE), bf16),
        pltpu.VMEM((OWNERS, tiles * modes, LANES), bf16),
        pltpu.VMEM((n, tiles * modes, LANES), bf16),
        pltpu.VMEM((n, tiles * modes, LANES), bf16),
        pltpu.VMEM((OWNERS, tiles * modes, LANES), bf16),
        pltpu.SemaphoreType.DMA((16,)),
        pltpu.SemaphoreType.DMA((chunks,)),
        pltpu.SemaphoreType.DMA((chunks,)),
        pltpu.SemaphoreType.DMA((chunks,)),
        pltpu.SemaphoreType.DMA((chunks,)),
        pltpu.SemaphoreType.DMA((1,)),
        pltpu.SemaphoreType.DMA((n,)),
        pltpu.SemaphoreType.DMA((1,)),
        pltpu.SemaphoreType.DMA((OWNERS,)),
        pltpu.SemaphoreType.REGULAR,
    ]
    return pl.pallas_call(
        functools.partial(kernel, n, minor, nodes),
        out_shape=jax.ShapeDtypeStruct((rows, channels), bf16),
        in_specs=[pl.BlockSpec(memory_space=pltpu.HBM)] * len(operands),
        out_specs=pl.BlockSpec(memory_space=pltpu.VMEM),
        scratch_shapes=scratch,
        compiler_params=pltpu.CompilerParams(
            collective_id=0, has_side_effects=True, vmem_limit_bytes=60 * 1024 * 1024
        ),
    )(*operands)


def solution(mesh):
    s, r = P(axes, None), P()
    specs = (s, s, s, r, r, r, s, s, r, r, r, r)
    return jax.shard_map(local, mesh=mesh, in_specs=specs, out_specs=s, check_vma=False)
```

```python
import functools

import jax
import jax.numpy as jnp
import ml_dtypes
import numpy as np
from jax import lax
from jax.experimental import pallas as pl
from jax.experimental.pallas import tpu as pltpu
from jax.sharding import PartitionSpec as P

axes = ("seqmaj", "seqmin")
MESH = pl.DeviceIdType.MESH
f32, bf16 = jnp.float32, jnp.bfloat16
WIDE = 512
NARROW = 256
LANES = 128
NODES = 16
OWNERS = 8


def owner_places(n, minor):
    order = sorted((i, -c) for i in range(minor // 2) for c in range(n // minor))
    return sorted(2 * i - c * minor for i, c in order[:OWNERS])


def split(table):
    high = table.astype(ml_dtypes.bfloat16).astype(np.float64)
    return high, table - high


def tables(rows):
    size = 2 * rows
    theta = 2.0 * np.pi * (np.arange(rows) + 0.5) / size
    angle = theta[:, None] * np.arange(size)[None, :]
    forward = np.concatenate([np.cos(angle), np.sin(angle)], axis=0)
    inverse = forward.T / rows
    nodes = 0.5 * (rows - 1) * (1.0 - np.cos(np.pi * (np.arange(NODES) + 0.5) / NODES))
    t = np.arange(rows, dtype=np.float64)
    basis = np.stack([
        np.prod([(t - nodes[m]) / (nodes[k] - nodes[m]) for m in range(NODES) if m != k], axis=0) for k in range(NODES)
    ], axis=1)
    high, low = split(basis)
    expand = np.concatenate([high, high, low], axis=1)
    moments = np.concatenate([high[::-1].T, low[::-1].T], axis=0)
    high, low = split(forward[:, :rows] @ basis)
    lift = np.concatenate([high, high, low], axis=1)
    at = np.broadcast_to(nodes[:, None], (NODES, LANES))
    return [jnp.asarray(a, bf16) for a in (forward, inverse, expand, moments, lift)] + [jnp.asarray(at, f32)], nodes


def mm(a, b):
    return jnp.dot(a, b, preferred_element_type=f32)


def spectral_product(x, h):
    half = x.shape[0] // 2
    xc, xs, hc, hs = x[:half], x[half:], h[:half], h[half:]
    return jnp.concatenate([xc * hc - xs * hs, xc * hs + xs * hc], axis=0).astype(bf16)


def stacked(x):
    high = x.astype(bf16)
    low = (x - high.astype(f32)).astype(bf16)
    return jnp.concatenate([high, low, high], axis=0)


def kernel(
    n, minor, nodes,
    q1h, k1h, v1h, tapsh, skip1h, w1h, q2h, k2h, resh, rateh, skip2h, w2h, fwdh, invh, expandh, momh, lifth, ath, out,
    q1, k1, v1, taps, skip1, w1, q2, k2, res, rate, skip2, w2, fwd, inv, expand, mom, lift, at,
    win, h1, h2, by_node, by_mode, coef, hop, scale, start, acc, y, g2, ends, mate, got, sout, sin,
    in_sem, w1_sem, w2_sem, bsend, brecv, esend, erecv, msend, mrecv, ssend, srecv, ready,
):
    rows, channels = q1.shape
    modes = rate.shape[0]
    chunks = channels // WIDE
    pieces = channels // NARROW
    owners = ends.shape[0]
    tiles = ends.shape[1] // modes
    me = lax.axis_index("seqmaj") * minor + lax.axis_index("seqmin")
    homes = owner_places(n, minor)
    mine = functools.reduce(lambda m, j: jnp.where(me == homes[j], j, m), range(owners), 0)
    owner = functools.reduce(jnp.logical_or, [me == home for home in homes])
    odd = lax.rem(me, 2) == 1

    def place(d):
        return (lax.div(d, minor), lax.rem(d, minor))

    barrier = pltpu.get_barrier_semaphore()

    @pl.when(me > 0)
    def _():
        @pl.when(jnp.logical_not(functools.reduce(jnp.logical_or, [me - 1 == home for home in homes])))
        def _():
            pl.semaphore_signal(barrier, inc=1, device_id=place(me - 1), device_id_type=MESH)

    loads = {}
    for i, (name, src, dst) in enumerate([
        ("k1", k1h, k1), ("v1", v1h, v1), ("rate", rateh, rate), ("res", resh, res), ("at", ath, at), ("fwd", fwdh, fwd),
        ("taps", tapsh, taps), ("lift", lifth, lift), ("inv", invh, inv), ("q1", q1h, q1), ("skip1", skip1h, skip1),
        ("k2", k2h, k2), ("skip2", skip2h, skip2), ("q2", q2h, q2), ("mom", momh, mom), ("expand", expandh, expand),
    ]):
        loads[name] = pltpu.make_async_copy(src, dst, in_sem.at[i])
        loads[name].start()

    def weight_load(src, dst, sem, c):
        return pltpu.make_async_copy(src.at[pl.ds(c * WIDE, WIDE), :], dst.at[pl.ds(c * WIDE, WIDE), :], sem.at[c])

    for c in range(chunks):
        weight_load(w1h, w1, w1_sem, c).start()

    for home in homes:

        @pl.when(me != home)
        def _():
            pl.semaphore_signal(barrier, inc=1, device_id=(home // minor, home % minor), device_id_type=MESH)

    for c in range(chunks):
        weight_load(w2h, w2, w2_sem, c).start()

    def cols(c):
        return slice(c * WIDE, (c + 1) * WIDE)

    def border(c):
        return pltpu.make_async_remote_copy(
            src_ref=win.at[c, pl.ds(rows, rows), :], dst_ref=win.at[c, pl.ds(0, rows), :],
            send_sem=bsend.at[c], recv_sem=brecv.at[c],
            device_id=place(lax.rem(me + 1, n)), device_id_type=MESH,
        )

    def thin(p):
        return slice(p * NARROW, (p + 1) * NARROW)

    early = jnp.logical_and(jnp.logical_not(owner), me < n - 1)
    loads["k1"].wait()
    loads["v1"].wait()
    for c in range(chunks):
        for p in (2 * c, 2 * c + 1):
            win[p, rows:, :] = (k1[:, thin(p)].astype(f32) * v1[:, thin(p)].astype(f32)).astype(bf16)

        @pl.when(early)
        def _():
            if c == 0:
                pl.semaphore_wait(barrier, 1)
            border(2 * c).start()
            border(2 * c + 1).start()

    @pl.when(me == 0)
    def _():
        for p in range(pieces):
            win[p, :rows, :] = jnp.zeros((rows, NARROW), bf16)

    loads["rate"].wait()
    loads["res"].wait()
    loads["at"].wait()

    @pl.loop(0, channels // LANES)
    def _(b):
        lane = pl.ds(pl.multiple_of(b * LANES, LANES), LANES)
        lam = rate[:, lane]
        weight = res[:, lane] * jnp.sqrt(lam)
        for k in range(NODES):
            by_node[k, :, lane] = jnp.exp(lam * (-float(nodes[k])))
        total = jnp.zeros((NODES, LANES), f32)
        where = at[...]
        for r in range(modes):
            value = jnp.exp(-(jnp.broadcast_to(lam[r : r + 1], (NODES, LANES)) * where))
            by_mode[r, :, lane] = value
            total = total + value * jnp.broadcast_to(weight[r : r + 1], (NODES, LANES))
        coef[:, lane] = total
        hop[:, lane] = jnp.exp(lam * (-float(rows)))
        scale[:, lane] = weight * jnp.exp(-lam)

    loads["fwd"].wait()
    loads["taps"].wait()
    loads["lift"].wait()

    for c in range(chunks):
        for p in (2 * c, 2 * c + 1):
            h1[p] = mm(fwd[:, :rows], taps[:, thin(p)])
        h2[c] = mm(lift[...], stacked(coef[:, cols(c)]))

    @pl.when(owner)
    def _():
        pl.semaphore_wait(barrier, n - 1)
        @pl.when(me < n - 1)
        def _():
            for p in range(pieces):
                border(p).start()

        @pl.loop(1, n)
        def _(p):
            pl.semaphore_signal(ready, inc=1, device_id=place(lax.rem(me + p, n)), device_id_type=MESH)

    loads["inv"].wait()
    loads["q1"].wait()
    loads["skip1"].wait()

    def first_act(group):
        @pl.when(me > 0)
        def _():
            for p in group:
                border(p).wait_recv()

        acts = []
        for p in group:
            spec = spectral_product(mm(fwd[...], win[p]), h1[p])
            short = mm(inv[rows:, :], spec)
            own = win[p, rows:, :].astype(f32)
            acts.append((q1[:, thin(p)].astype(f32) * (short + skip1[:, thin(p)] * own)).astype(bf16))
        return jnp.concatenate(acts, axis=1)

    for c in range(chunks):
        weight_load(w1h, w1, w1_sem, c).wait()
    groups = [(p, p + 1) for p in range(0, pieces - 2, 2)] + [(pieces - 2,), (pieces - 1,)]
    for group in groups[:-1]:
        act = first_act(group)
        part = mm(act, w1[group[0] * NARROW : (group[-1] + 1) * NARROW, :])
        if group[0] == 0:
            acc[...] = part
        else:
            acc[...] += part

    last = chunks - 1
    act = first_act(groups[-1])
    loads["k2"].wait()
    loads["mom"].wait()

    @pl.when(owner)
    def _():
        pl.semaphore_wait(ready, owners - 1)

    @pl.when(jnp.logical_not(owner))
    def _():
        pl.semaphore_wait(ready, owners)

    per_chunk = WIDE // LANES
    for c in range(chunks):
        v = acc[:, cols(c)] + mm(act, w1[thin(pieces - 1), cols(c)])
        gated = (k2[:, cols(c)].astype(f32) * v.astype(bf16).astype(f32)).astype(bf16)
        g2[c] = gated
        moment = mm(mom[...], gated)
        moment = moment[:NODES] + moment[NODES:]
        e = jnp.zeros((modes, WIDE), f32)
        for k in range(NODES):
            e = e + by_node[k, :, cols(c)] * jnp.broadcast_to(moment[k : k + 1], (modes, WIDE))
        for i in range(per_chunk):
            o, s = divmod(c * per_chunk + i, tiles)
            ends[o, s * modes : (s + 1) * modes, :] = e[:, i * LANES : (i + 1) * LANES].astype(bf16)

    def ends_copy(j):
        return pltpu.make_async_remote_copy(
            src_ref=ends.at[j], dst_ref=got.at[me], send_sem=esend.at[0], recv_sem=erecv.at[me],
            device_id=(homes[j] // minor, homes[j] % minor), device_id_type=MESH,
        )

    mate_copy = pltpu.make_async_remote_copy(
        src_ref=ends, dst_ref=mate, send_sem=msend.at[0], recv_sem=mrecv.at[0],
        device_id=place(lax.rem(me + 1, n)), device_id_type=MESH,
    )

    @pl.when(me < n - 2)
    def _():
        for j in range(owners):

            @pl.when(me != homes[j])
            def _():
                ends_copy(j).start()

    @pl.when(jnp.logical_not(odd))
    def _():
        mate_copy.start()

    def state_copy(d):
        return pltpu.make_async_remote_copy(
            src_ref=sout.at[lax.div(d, 2)], dst_ref=sin.at[mine], send_sem=ssend.at[0], recv_sem=srecv.at[mine],
            device_id=place(d), device_id_type=MESH,
        )

    def scan_and_serve():
        got[me] = ends[mine]
        decays, scales = [], []
        for s in range(tiles):
            lane = pl.ds(pl.multiple_of((mine * tiles + s) * LANES, LANES), LANES)
            decays.append(hop[:, lane])
            scales.append(scale[:, lane])
        decay, weight = jnp.concatenate(decays, axis=0), jnp.concatenate(scales, axis=0)

        def take(p):
            @pl.when(p != me)
            def _():
                pltpu.make_async_remote_copy(
                    src_ref=ends.at[0], dst_ref=got.at[p], send_sem=esend.at[0], recv_sem=erecv.at[p],
                    device_id=place(lax.rem(me + 1, n)), device_id_type=MESH,
                ).wait_recv()

        def serve(chip, state):
            take(2 * chip)
            take(2 * chip + 1)
            state = (state * decay + got[2 * chip].astype(f32)) * decay + got[2 * chip + 1].astype(f32)
            sout[chip + 1] = (state * weight).astype(bf16)

            @pl.when(2 * chip + 2 != me)
            def _():
                state_copy(2 * chip + 2).start()

            @pl.when(2 * chip + 2 == me)
            def _():
                sin[mine] = sout[chip + 1]

            state_copy(2 * chip + 3).start()
            return state

        lax.fori_loop(0, n // 2 - 1, serve, jnp.zeros((tiles * modes, LANES), f32))

    pl.when(jnp.logical_and(owner, me > 0))(scan_and_serve)

    loads["skip2"].wait()
    for c in range(chunks):
        gated = g2[c]
        spec = spectral_product(mm(fwd[:, :rows], gated), h2[c])
        y[c] = mm(inv[:rows, :], spec) + skip2[:, cols(c)] * gated.astype(f32)

    loads["q2"].wait()
    loads["expand"].wait()

    @pl.when(me < 2)
    def _():
        sin[...] = jnp.zeros_like(sin)

    @pl.when(me >= 2)
    def _():
        for j in range(owners):

            @pl.when(me != homes[j])
            def _():
                pltpu.make_async_remote_copy(
                    src_ref=sout.at[0], dst_ref=sin.at[j], send_sem=ssend.at[0], recv_sem=srecv.at[j],
                    device_id=place(lax.rem(me + 1, n)), device_id_type=MESH,
                ).wait_recv()

    @pl.when(odd)
    def _():
        mate_copy.wait_recv()

    @pl.when(jnp.logical_not(odd))
    def _():
        mate[...] = jnp.zeros_like(mate)

    for b in range(chunks * per_chunk):
        o, s = divmod(b, tiles)
        lane, part = slice(b * LANES, (b + 1) * LANES), slice(s * modes, (s + 1) * modes)
        before = sin[o, part, :].astype(f32)
        after = before * hop[:, lane] + scale[:, lane] * mate[o, part, :].astype(f32)
        start[:, lane] = jnp.where(odd, after, before)

    def second_act(c):
        total = jnp.zeros((NODES, WIDE), f32)
        for r in range(modes):
            total = total + by_mode[r, :, cols(c)] * jnp.broadcast_to(start[r : r + 1, cols(c)], (NODES, WIDE))
        return (q2[:, cols(c)].astype(f32) * (y[c] + mm(expand[...], stacked(total)))).astype(bf16)

    for c in range(chunks):
        weight_load(w2h, w2, w2_sem, c).wait()
    for c in range(chunks):
        act = second_act(c)
        if c == 0:
            acc[...] = mm(act, w2[cols(c), :])
        elif c < last:
            acc[...] += mm(act, w2[cols(c), :])
        else:
            out[...] = (acc[...] + mm(act, w2[cols(c), :])).astype(bf16)

    pl.when(jnp.logical_and(owner, me == 0))(scan_and_serve)

    @pl.when(me < n - 1)
    def _():
        for p in range(pieces):
            border(p).wait_send()

    def sent(src, dst, count, send_sem, recv_sem):
        span = pl.ds(0, count)
        pltpu.make_async_remote_copy(
            src_ref=src.at[span], dst_ref=dst.at[span], send_sem=send_sem.at[0], recv_sem=recv_sem.at[0],
            device_id=place(lax.rem(me + 1, n)), device_id_type=MESH,
        ).wait_send()

    @pl.when(jnp.logical_not(odd))
    def _():
        mate_copy.wait_send()

    @pl.when(jnp.logical_and(me < n - 2, jnp.logical_not(owner)))
    def _():
        sent(ends, got, owners, esend, erecv)

    @pl.when(jnp.logical_and(me < n - 2, owner))
    def _():
        sent(ends, got, owners - 1, esend, erecv)

    @pl.when(owner)
    def _():
        sent(sout, got, n // 2 - 2, ssend, srecv)

        @pl.when(me == 0)
        def _():
            sent(sout, got, n // 2, ssend, srecv)

        @pl.when(me > 0)
        def _():
            sent(sout, got, n // 2 - 1, ssend, srecv)


def store(src, dst, sem):
    part = src.shape[0] // sem.shape[0]
    copies = [
        pltpu.make_async_copy(src.at[pl.ds(i * part, part)], dst.at[pl.ds(i * part, part)], sem.at[i])
        for i in range(sem.shape[0])
    ]
    for copy in copies:
        copy.start()
    for copy in copies:
        copy.wait()


def local(q1, k1, v1, taps, skip1, w1, q2, k2, residue, rate, skip2, w2):
    rows, channels = q1.shape
    modes = rate.shape[0]
    minor = lax.axis_size("seqmin")
    n = lax.axis_size("seqmaj") * minor
    constants, nodes = tables(rows)
    operands = (q1, k1, v1, taps, skip1[None], w1, q2, k2, residue, rate, skip2[None], w2, *constants)
    operands = [pltpu.with_memory_space_constraint(a, pltpu.HBM) for a in operands]
    chunks, pieces, tiles = channels // WIDE, channels // NARROW, channels // (LANES * OWNERS)
    scratch = [pltpu.VMEM(a.shape, a.dtype) for a in operands] + [
        pltpu.VMEM((pieces, 2 * rows, NARROW), bf16),
        pltpu.VMEM((pieces, 2 * rows, NARROW), f32),
        pltpu.VMEM((chunks, 2 * rows, WIDE), f32),
        pltpu.VMEM((NODES, modes, channels), f32),
        pltpu.VMEM((modes, NODES, channels), f32),
        pltpu.VMEM((NODES, channels), f32),
        pltpu.VMEM((modes, channels), f32),
        pltpu.VMEM((modes, channels), f32),
        pltpu.VMEM((modes, channels), f32),
        pltpu.VMEM((rows, channels), f32),
        pltpu.VMEM((chunks, rows, WIDE), f32),
        pltpu.VMEM((chunks, rows, WIDE), bf16),
        pltpu.VMEM((OWNERS, tiles * modes, LANES), bf16),
        pltpu.VMEM((OWNERS, tiles * modes, LANES), bf16),
        pltpu.VMEM((n, tiles * modes, LANES), bf16),
        pltpu.VMEM((n // 2, tiles * modes, LANES), bf16),
        pltpu.VMEM((OWNERS, tiles * modes, LANES), bf16),
        pltpu.SemaphoreType.DMA((16,)),
        pltpu.SemaphoreType.DMA((chunks,)),
        pltpu.SemaphoreType.DMA((chunks,)),
        pltpu.SemaphoreType.DMA((pieces,)),
        pltpu.SemaphoreType.DMA((pieces,)),
        pltpu.SemaphoreType.DMA((1,)),
        pltpu.SemaphoreType.DMA((n,)),
        pltpu.SemaphoreType.DMA((1,)),
        pltpu.SemaphoreType.DMA((1,)),
        pltpu.SemaphoreType.DMA((1,)),
        pltpu.SemaphoreType.DMA((OWNERS,)),
        pltpu.SemaphoreType.REGULAR,
    ]
    mixed = pl.pallas_call(
        functools.partial(kernel, n, minor, nodes),
        out_shape=pltpu.VMEM((rows, channels), bf16),
        in_specs=[pl.BlockSpec(memory_space=pltpu.HBM)] * len(operands),
        out_specs=pl.BlockSpec(memory_space=pltpu.VMEM),
        scratch_shapes=scratch,
        compiler_params=pltpu.CompilerParams(
            collective_id=0, has_side_effects=True, vmem_limit_bytes=56 * 1024 * 1024
        ),
    )(*operands)
    return pl.pallas_call(
        store,
        out_shape=jax.ShapeDtypeStruct((rows, channels), bf16),
        in_specs=[pl.BlockSpec(memory_space=pl.ANY)],
        out_specs=pl.BlockSpec(memory_space=pl.ANY),
        scratch_shapes=[pltpu.SemaphoreType.DMA((4,))],
    )(pltpu.with_memory_space_constraint(mixed, pltpu.VMEM))


def solution(mesh):
    s, r = P(axes, None), P()
    specs = (s, s, s, r, r, r, s, s, r, r, r, r)
    return jax.shard_map(local, mesh=mesh, in_specs=specs, out_specs=s, check_vma=False)
```

```python
import functools

import jax
import jax.numpy as jnp
import ml_dtypes
import numpy as np
from jax import lax
from jax.experimental import pallas as pl
from jax.experimental.pallas import tpu as pltpu
from jax.sharding import PartitionSpec as P

axes = ("seqmaj", "seqmin")
MESH = pl.DeviceIdType.MESH
f32, bf16 = jnp.float32, jnp.bfloat16
WIDE = 512
NARROW = 256
LANES = 128
NODES = 16
OWNERS = 8


def owner_places(n, minor):
    order = sorted((i, -c) for i in range(minor // 2) for c in range(n // minor))
    return sorted(2 * i - c * minor for i, c in order[:OWNERS])


def split(table):
    high = table.astype(ml_dtypes.bfloat16).astype(np.float64)
    return high, table - high


def tables(rows):
    size = 2 * rows
    theta = 2.0 * np.pi * (np.arange(rows) + 0.5) / size
    angle = theta[:, None] * np.arange(size)[None, :]
    forward = np.concatenate([np.cos(angle), np.sin(angle)], axis=0)
    inverse = forward.T / rows
    nodes = 0.5 * (rows - 1) * (1.0 - np.cos(np.pi * (np.arange(NODES) + 0.5) / NODES))
    t = np.arange(rows, dtype=np.float64)
    basis = np.stack([
        np.prod([(t - nodes[m]) / (nodes[k] - nodes[m]) for m in range(NODES) if m != k], axis=0) for k in range(NODES)
    ], axis=1)
    high, low = split(basis)
    expand = np.concatenate([high, high, low], axis=1)
    moments = np.concatenate([high[::-1].T, low[::-1].T], axis=0)
    high, low = split(forward[:, :rows] @ basis)
    lift = np.concatenate([high, high, low], axis=1)
    parts = [np.pad(a, ((0, 0), (0, size - a.shape[1]))) for a in (forward, inverse, lift, expand, moments)]
    return jnp.asarray(np.concatenate(parts, axis=0), bf16), nodes


def mm(a, b):
    return jnp.dot(a, b, preferred_element_type=f32)


def spectral_product(x, h):
    half = x.shape[0] // 2
    xc, xs, hc, hs = x[:half], x[half:], h[:half], h[half:]
    return jnp.concatenate([xc * hc - xs * hs, xc * hs + xs * hc], axis=0).astype(bf16)


def stacked(x):
    high = x.astype(bf16)
    low = (x - high.astype(f32)).astype(bf16)
    return jnp.concatenate([high, low, high], axis=0)


def kernel(
    n, minor, nodes,
    q1h, k1h, v1h, tapsh, skip1h, w1h, q2h, k2h, resh, rateh, skip2h, w2h, tableh, out,
    kv, rates, table, acts, skips, w1, w2,
    win, h1, h2, by_node, by_mode, coef, hop, scale, start, acc, y, g2, ends, mate, got, sout, sin,
    load_sem, brecv, erecv, mrecv, srecv, sent, ready,
):
    k1, v1 = kv.at[0], kv.at[1]
    rate, res = rates.at[0], rates.at[1]
    taps, q1, k2, q2 = (acts.at[i] for i in range(4))
    skip1, skip2 = skips.at[0], skips.at[1]
    rows, channels = q1h.shape
    modes = rateh.shape[0]
    size = 2 * rows
    fwd, inv = table.at[pl.ds(0, size), :], table.at[pl.ds(size, size), :]
    lift = table.at[pl.ds(2 * size, size), pl.ds(0, 3 * NODES)]
    expand = table.at[pl.ds(3 * size, rows), pl.ds(0, 3 * NODES)]
    mom = table.at[pl.ds(3 * size + rows, 2 * NODES), pl.ds(0, rows)]
    chunks = channels // WIDE
    pieces = channels // NARROW
    owners = ends.shape[0]
    tiles = ends.shape[1] // modes
    me = lax.axis_index("seqmaj") * minor + lax.axis_index("seqmin")
    homes = owner_places(n, minor)
    mine = functools.reduce(lambda m, j: jnp.where(me == homes[j], j, m), range(owners), 0)
    owner = functools.reduce(jnp.logical_or, [me == home for home in homes])
    odd = lax.rem(me, 2) == 1

    def place(d):
        return (lax.div(d, minor), lax.rem(d, minor))

    barrier = pltpu.get_barrier_semaphore()

    @pl.when(me > 0)
    def _():
        @pl.when(jnp.logical_not(functools.reduce(jnp.logical_or, [me - 1 == home for home in homes])))
        def _():
            pl.semaphore_signal(barrier, inc=1, device_id=place(me - 1), device_id_type=MESH)

    def loads(sem, copies):
        for src, dst in copies:
            pltpu.make_async_copy(src, dst, load_sem.at[sem]).start()

    def loaded(sem, whole):
        pltpu.make_async_copy(whole, whole, load_sem.at[sem]).wait()

    def weight_loads(sem, src, dst):
        spans = [pl.ds(c * WIDE, WIDE) for c in range(chunks)]
        loads(sem, [(src.at[span, :], dst.at[span, :]) for span in spans])

    loads(0, [(k1h, k1), (v1h, v1)])
    loads(1, [(rateh, rate), (resh, res)])
    loads(2, [(tableh, table)])
    loads(3, [(tapsh, taps), (q1h, q1), (k2h, k2), (q2h, q2)])
    loads(4, [(skip1h, skip1), (skip2h, skip2)])
    weight_loads(5, w1h, w1)

    for home in homes:

        @pl.when(me != home)
        def _():
            pl.semaphore_signal(barrier, inc=1, device_id=(home // minor, home % minor), device_id_type=MESH)

    weight_loads(6, w2h, w2)

    def cols(c):
        return slice(c * WIDE, (c + 1) * WIDE)

    def border(c):
        return pltpu.make_async_remote_copy(
            src_ref=win.at[c, pl.ds(rows, rows), :], dst_ref=win.at[c, pl.ds(0, rows), :],
            send_sem=sent.at[0], recv_sem=brecv.at[min(c // 2, chunks - 1) + (1 if c == pieces - 1 else 0)],
            device_id=place(lax.rem(me + 1, n)), device_id_type=MESH,
        )

    def thin(p):
        return slice(p * NARROW, (p + 1) * NARROW)

    early = jnp.logical_and(jnp.logical_not(owner), me < n - 1)
    loaded(0, kv)
    for c in range(chunks):
        for p in (2 * c, 2 * c + 1):
            win[p, rows:, :] = (k1[:, thin(p)].astype(f32) * v1[:, thin(p)].astype(f32)).astype(bf16)

        @pl.when(early)
        def _():
            if c == 0:
                pl.semaphore_wait(barrier, 1)
            border(2 * c).start()
            border(2 * c + 1).start()

    @pl.when(me == 0)
    def _():
        for p in range(pieces):
            win[p, :rows, :] = jnp.zeros((rows, NARROW), bf16)

    loaded(1, rates)
    index = lax.broadcasted_iota(jnp.int32, (NODES, LANES), 0)
    place_of = functools.reduce(lambda x, k: jnp.where(index == k, float(nodes[k]), x), range(NODES), jnp.zeros((NODES, LANES), f32))

    @pl.loop(0, channels // LANES)
    def _(b):
        lane = pl.ds(pl.multiple_of(b * LANES, LANES), LANES)
        lam = rate[:, lane]
        weight = res[:, lane] * jnp.sqrt(lam)
        for k in range(NODES):
            by_node[k, :, lane] = jnp.exp(lam * (-float(nodes[k])))
        total = jnp.zeros((NODES, LANES), f32)
        for r in range(modes):
            value = jnp.exp(-(jnp.broadcast_to(lam[r : r + 1], (NODES, LANES)) * place_of))
            by_mode[r, :, lane] = value
            total = total + value * jnp.broadcast_to(weight[r : r + 1], (NODES, LANES))
        coef[:, lane] = total
        hop[:, lane] = jnp.exp(lam * (-float(rows)))
        scale[:, lane] = weight * jnp.exp(-lam)

    loaded(2, table)
    loaded(3, acts)
    loaded(4, skips)

    for c in range(chunks):
        for p in (2 * c, 2 * c + 1):
            h1[p] = mm(fwd[:, :rows], taps[:, thin(p)])
        h2[c] = mm(lift[...], stacked(coef[:, cols(c)]))

    @pl.when(owner)
    def _():
        pl.semaphore_wait(barrier, n - 1)
        @pl.when(me < n - 1)
        def _():
            for p in range(pieces):
                border(p).start()

        @pl.loop(1, n)
        def _(p):
            pl.semaphore_signal(ready, inc=1, device_id=place(lax.rem(me + p, n)), device_id_type=MESH)

    def first_act(group):
        @pl.when(me > 0)
        def _():
            part = pl.ds(group[0], len(group))
            whole = win.at[part, pl.ds(0, rows), :]
            pltpu.make_async_copy(whole, whole, brecv.at[groups.index(group)]).wait()

        acts = []
        for p in group:
            spec = spectral_product(mm(fwd[...], win[p]), h1[p])
            short = mm(inv[rows:, :], spec)
            own = win[p, rows:, :].astype(f32)
            acts.append((q1[:, thin(p)].astype(f32) * (short + skip1[:, thin(p)] * own)).astype(bf16))
        return jnp.concatenate(acts, axis=1)

    loaded(5, w1)
    groups = [(p, p + 1) for p in range(0, pieces - 2, 2)] + [(pieces - 2,), (pieces - 1,)]
    for group in groups[:-1]:
        act = first_act(group)
        part = mm(act, w1[group[0] * NARROW : (group[-1] + 1) * NARROW, :])
        if group[0] == 0:
            acc[...] = part
        else:
            acc[...] += part

    act = first_act(groups[-1])
    @pl.when(owner)
    def _():
        pl.semaphore_wait(ready, owners - 1)

    @pl.when(jnp.logical_not(owner))
    def _():
        pl.semaphore_wait(ready, owners)

    per_chunk = WIDE // LANES
    for c in range(chunks):
        v = acc[:, cols(c)] + mm(act, w1[thin(pieces - 1), cols(c)])
        g2[c] = (k2[:, cols(c)].astype(f32) * v.astype(bf16).astype(f32)).astype(bf16)
    for c in range(chunks):
        moment = mm(mom[...], g2[c])
        coef[:, cols(c)] = moment[:NODES] + moment[NODES:]
    for c in range(chunks):
        e = jnp.zeros((modes, WIDE), f32)
        for k in range(NODES):
            e = e + by_node[k, :, cols(c)] * jnp.broadcast_to(coef[k : k + 1, cols(c)], (modes, WIDE))
        for i in range(per_chunk):
            o, s = divmod(c * per_chunk + i, tiles)
            ends[o, s * modes : (s + 1) * modes, :] = e[:, i * LANES : (i + 1) * LANES].astype(bf16)

    def ends_copy(j):
        return pltpu.make_async_remote_copy(
            src_ref=ends.at[j], dst_ref=got.at[me], send_sem=sent.at[0], recv_sem=erecv.at[lax.div(me, 2)],
            device_id=(homes[j] // minor, homes[j] % minor), device_id_type=MESH,
        )

    mate_copy = pltpu.make_async_remote_copy(
        src_ref=ends, dst_ref=mate, send_sem=sent.at[0], recv_sem=mrecv.at[0],
        device_id=place(lax.rem(me + 1, n)), device_id_type=MESH,
    )

    @pl.when(me < n - 2)
    def _():
        for j in range(owners):

            @pl.when(me != homes[j])
            def _():
                ends_copy(j).start()

    @pl.when(jnp.logical_not(odd))
    def _():
        mate_copy.start()

    def state_copy(d):
        return pltpu.make_async_remote_copy(
            src_ref=sout.at[lax.div(d, 2)], dst_ref=sin.at[mine], send_sem=sent.at[0], recv_sem=srecv.at[0],
            device_id=place(d), device_id_type=MESH,
        )

    def scan_and_serve():
        got[me] = ends[mine]
        decays, scales = [], []
        for s in range(tiles):
            lane = pl.ds(pl.multiple_of((mine * tiles + s) * LANES, LANES), LANES)
            decays.append(hop[:, lane])
            scales.append(scale[:, lane])
        decay, weight = jnp.concatenate(decays, axis=0), jnp.concatenate(scales, axis=0)

        def serve(chip, state):
            @pl.when(2 * chip != me)
            def _():
                both = got.at[pl.ds(2 * chip, 2)]
                pltpu.make_async_copy(both, both, erecv.at[chip]).wait()

            @pl.when(2 * chip == me)
            def _():
                one = got.at[2 * chip + 1]
                pltpu.make_async_copy(one, one, erecv.at[chip]).wait()

            state = (state * decay + got[2 * chip].astype(f32)) * decay + got[2 * chip + 1].astype(f32)
            sout[chip + 1] = (state * weight).astype(bf16)

            @pl.when(2 * chip + 2 != me)
            def _():
                state_copy(2 * chip + 2).start()

            @pl.when(2 * chip + 2 == me)
            def _():
                sin[mine] = sout[chip + 1]

            state_copy(2 * chip + 3).start()
            return state

        lax.fori_loop(0, n // 2 - 1, serve, jnp.zeros((tiles * modes, LANES), f32))

    pl.when(jnp.logical_and(owner, me > 0))(scan_and_serve)

    for c in range(chunks):
        gated = g2[c]
        spec = spectral_product(mm(fwd[:, :rows], gated), h2[c])
        y[c] = mm(inv[:rows, :], spec) + skip2[:, cols(c)] * gated.astype(f32)

    @pl.when(me < 2)
    def _():
        sin[...] = jnp.zeros_like(sin)

    def states_in(count):
        some = sin.at[pl.ds(0, count)]
        pltpu.make_async_copy(some, some, srecv.at[0]).wait()

    @pl.when(jnp.logical_and(me >= 2, owner))
    def _():
        states_in(owners - 1)

    @pl.when(jnp.logical_and(me >= 2, jnp.logical_not(owner)))
    def _():
        states_in(owners)

    @pl.when(odd)
    def _():
        mate_copy.wait_recv()

    @pl.when(jnp.logical_not(odd))
    def _():
        mate[...] = jnp.zeros_like(mate)

    for b in range(chunks * per_chunk):
        o, s = divmod(b, tiles)
        lane, part = slice(b * LANES, (b + 1) * LANES), slice(s * modes, (s + 1) * modes)
        before = sin[o, part, :].astype(f32)
        after = before * hop[:, lane] + scale[:, lane] * mate[o, part, :].astype(f32)
        start[:, lane] = jnp.where(odd, after, before)

    loaded(6, w2)
    for c in range(chunks):
        total = jnp.zeros((NODES, WIDE), f32)
        for r in range(modes):
            total = total + by_mode[r, :, cols(c)] * jnp.broadcast_to(start[r : r + 1, cols(c)], (NODES, WIDE))
        coef[:, cols(c)] = total
    for c in range(chunks):
        long = y[c] + mm(expand[...], stacked(coef[:, cols(c)]))
        g2[c] = (q2[:, cols(c)].astype(f32) * long).astype(bf16)
    for c in range(chunks):
        part = mm(g2[c], w2[cols(c), :])
        if c == 0:
            acc[...] = part
        elif c < chunks - 1:
            acc[...] += part
        else:
            out[...] = (acc[...] + part).astype(bf16)

    pl.when(jnp.logical_and(owner, me == 0))(scan_and_serve)

    def left(whole):
        pltpu.make_async_copy(whole, whole, sent.at[0]).wait()

    @pl.when(me < n - 1)
    def _():
        left(win.at[:, pl.ds(0, rows), :])

    @pl.when(jnp.logical_not(odd))
    def _():
        left(ends)

    @pl.when(jnp.logical_and(me < n - 2, jnp.logical_not(owner)))
    def _():
        left(ends)

    @pl.when(jnp.logical_and(me < n - 2, owner))
    def _():
        left(ends.at[pl.ds(0, owners - 1)])

    @pl.when(owner)
    def _():
        left(sout.at[pl.ds(0, n // 2 - 2)])

        @pl.when(me < 2)
        def _():
            left(sout)

        @pl.when(me >= 2)
        def _():
            left(sout.at[pl.ds(0, n // 2 - 1)])


def store(src, dst, sem):
    part = src.shape[0] // sem.shape[0]
    copies = [
        pltpu.make_async_copy(src.at[pl.ds(i * part, part)], dst.at[pl.ds(i * part, part)], sem.at[i])
        for i in range(sem.shape[0])
    ]
    for copy in copies:
        copy.start()
    for copy in copies:
        copy.wait()


def local(q1, k1, v1, taps, skip1, w1, q2, k2, residue, rate, skip2, w2):
    rows, channels = q1.shape
    modes = rate.shape[0]
    minor = lax.axis_size("seqmin")
    n = lax.axis_size("seqmaj") * minor
    table, nodes = tables(rows)
    operands = (q1, k1, v1, taps, skip1[None], w1, q2, k2, residue, rate, skip2[None], w2, table)
    operands = [pltpu.with_memory_space_constraint(a, pltpu.HBM) for a in operands]
    chunks, pieces, tiles = channels // WIDE, channels // NARROW, channels // (LANES * OWNERS)
    scratch = [
        pltpu.VMEM((2, rows, channels), bf16),
        pltpu.VMEM((2, modes, channels), f32),
        pltpu.VMEM(table.shape, bf16),
        pltpu.VMEM((4, rows, channels), bf16),
        pltpu.VMEM((2, 1, channels), f32),
        pltpu.VMEM(w1.shape, bf16),
        pltpu.VMEM(w2.shape, bf16),
        pltpu.VMEM((pieces, 2 * rows, NARROW), bf16),
        pltpu.VMEM((pieces, 2 * rows, NARROW), f32),
        pltpu.VMEM((chunks, 2 * rows, WIDE), f32),
        pltpu.VMEM((NODES, modes, channels), f32),
        pltpu.VMEM((modes, NODES, channels), f32),
        pltpu.VMEM((NODES, channels), f32),
        pltpu.VMEM((modes, channels), f32),
        pltpu.VMEM((modes, channels), f32),
        pltpu.VMEM((modes, channels), f32),
        pltpu.VMEM((rows, channels), f32),
        pltpu.VMEM((chunks, rows, WIDE), f32),
        pltpu.VMEM((chunks, rows, WIDE), bf16),
        pltpu.VMEM((OWNERS, tiles * modes, LANES), bf16),
        pltpu.VMEM((OWNERS, tiles * modes, LANES), bf16),
        pltpu.VMEM((n, tiles * modes, LANES), bf16),
        pltpu.VMEM((n // 2, tiles * modes, LANES), bf16),
        pltpu.VMEM((OWNERS, tiles * modes, LANES), bf16),
        pltpu.SemaphoreType.DMA((7,)),
        pltpu.SemaphoreType.DMA((chunks + 1,)),
        pltpu.SemaphoreType.DMA((n // 2,)),
        pltpu.SemaphoreType.DMA((1,)),
        pltpu.SemaphoreType.DMA((1,)),
        pltpu.SemaphoreType.DMA((1,)),
        pltpu.SemaphoreType.REGULAR,
    ]
    mixed = pl.pallas_call(
        functools.partial(kernel, n, minor, nodes),
        out_shape=pltpu.VMEM((rows, channels), bf16),
        in_specs=[pl.BlockSpec(memory_space=pltpu.HBM)] * len(operands),
        out_specs=pl.BlockSpec(memory_space=pltpu.VMEM),
        scratch_shapes=scratch,
        compiler_params=pltpu.CompilerParams(
            collective_id=0, has_side_effects=True, vmem_limit_bytes=56 * 1024 * 1024
        ),
    )(*operands)
    return pl.pallas_call(
        store,
        out_shape=jax.ShapeDtypeStruct((rows, channels), bf16),
        in_specs=[pl.BlockSpec(memory_space=pl.ANY)],
        out_specs=pl.BlockSpec(memory_space=pl.ANY),
        scratch_shapes=[pltpu.SemaphoreType.DMA((1,))],
    )(pltpu.with_memory_space_constraint(mixed, pltpu.VMEM))


def solution(mesh):
    s, r = P(axes, None), P()
    specs = (s, s, s, r, r, r, s, s, r, r, r, r)
    return jax.shard_map(local, mesh=mesh, in_specs=specs, out_specs=s, check_vma=False)
```

```python
import functools

import jax
import jax.numpy as jnp
import ml_dtypes
import numpy as np
from jax import lax
from jax.experimental import pallas as pl
from jax.experimental.pallas import tpu as pltpu
from jax.sharding import PartitionSpec as P

axes = ("seqmaj", "seqmin")
MESH = pl.DeviceIdType.MESH
f32, bf16 = jnp.float32, jnp.bfloat16
WIDE = 512
NARROW = 256
LANES = 128
NODES = 16
OWNERS = 16


def owner_places(n, minor):
    order = sorted((i, -c) for i in range(minor // 2) for c in range(n // minor))
    return [2 * i - c * minor + core for i, c in reversed(order[: OWNERS // 2]) for core in range(2)]


def split(table):
    high = table.astype(ml_dtypes.bfloat16).astype(np.float64)
    return high, table - high


def tables(rows):
    size = 2 * rows
    theta = 2.0 * np.pi * (np.arange(rows) + 0.5) / size
    angle = theta[:, None] * np.arange(size)[None, :]
    forward = np.concatenate([np.cos(angle), np.sin(angle)], axis=0)
    inverse = forward.T / rows
    nodes = 0.5 * (rows - 1) * (1.0 - np.cos(np.pi * (np.arange(NODES) + 0.5) / NODES))
    t = np.arange(rows, dtype=np.float64)
    basis = np.stack([
        np.prod([(t - nodes[m]) / (nodes[k] - nodes[m]) for m in range(NODES) if m != k], axis=0) for k in range(NODES)
    ], axis=1)
    high, low = split(basis)
    expand = np.concatenate([high, high, low], axis=1)
    moments = np.concatenate([high[::-1].T, low[::-1].T], axis=0)
    high, low = split(forward[:, :rows] @ basis)
    lift = np.concatenate([high, high, low], axis=1)
    parts = [np.pad(a, ((0, 0), (0, size - a.shape[1]))) for a in (forward, inverse, lift, expand, moments)]
    return jnp.asarray(np.concatenate(parts, axis=0), bf16), nodes


def mm(a, b):
    return jnp.dot(a, b, preferred_element_type=f32)


def spectral_product(x, h):
    half = x.shape[0] // 2
    xc, xs, hc, hs = x[:half], x[half:], h[:half], h[half:]
    return jnp.concatenate([xc * hc - xs * hs, xc * hs + xs * hc], axis=0).astype(bf16)


def stacked(x):
    high = x.astype(bf16)
    low = (x - high.astype(f32)).astype(bf16)
    return jnp.concatenate([high, low, high], axis=0)


def kernel(
    n, minor, nodes,
    q1h, k1h, v1h, tapsh, skip1h, w1h, q2h, k2h, resh, rateh, skip2h, w2h, tableh, out,
    kv, rates, table, acts, skips, w1, w2,
    win, h1, h2, by_node, by_mode, coef, hop, scale, start, acc, y, g2, ends, mate, both, got, sout, sin,
    load_sem, brecv, erecv, mrecv, srecv, sent, ready,
):
    k1, v1 = kv.at[0], kv.at[1]
    rate, res = rates.at[0], rates.at[1]
    taps, q1, k2, q2 = (acts.at[i] for i in range(4))
    skip1, skip2 = skips.at[0], skips.at[1]
    rows, channels = q1h.shape
    modes = rateh.shape[0]
    size = 2 * rows
    fwd, inv = table.at[pl.ds(0, size), :], table.at[pl.ds(size, size), :]
    lift = table.at[pl.ds(2 * size, size), pl.ds(0, 3 * NODES)]
    expand = table.at[pl.ds(3 * size, rows), pl.ds(0, 3 * NODES)]
    mom = table.at[pl.ds(3 * size + rows, 2 * NODES), pl.ds(0, rows)]
    chunks = channels // WIDE
    pieces = channels // NARROW
    owners = ends.shape[0]
    tiles = ends.shape[1] // modes
    me = lax.axis_index("seqmaj") * minor + lax.axis_index("seqmin")
    homes = owner_places(n, minor)
    mine = functools.reduce(lambda m, j: jnp.where(me == homes[j], j, m), range(owners), 0)
    owner = functools.reduce(jnp.logical_or, [me == home for home in homes])
    odd = lax.rem(me, 2) == 1
    greeter = jnp.logical_and(owner, jnp.logical_not(odd))
    greeters = homes[::2]

    def place(d):
        return (lax.div(d, minor), lax.rem(d, minor))

    barrier = pltpu.get_barrier_semaphore()

    @pl.when(me > 0)
    def _():
        @pl.when(jnp.logical_not(functools.reduce(jnp.logical_or, [me - 1 == home for home in greeters])))
        def _():
            pl.semaphore_signal(barrier, inc=1, device_id=place(me - 1), device_id_type=MESH)

    def loads(sem, copies):
        for src, dst in copies:
            pltpu.make_async_copy(src, dst, load_sem.at[sem]).start()

    def loaded(sem, whole):
        pltpu.make_async_copy(whole, whole, load_sem.at[sem]).wait()

    def weight_loads(sem, src, dst):
        spans = [pl.ds(c * WIDE, WIDE) for c in range(chunks)]
        loads(sem, [(src.at[span, :], dst.at[span, :]) for span in spans])

    loads(0, [(k1h, k1), (v1h, v1)])
    loads(1, [(rateh, rate), (resh, res)])
    loads(2, [(tableh, table)])
    loads(3, [(tapsh, taps), (q1h, q1), (k2h, k2), (q2h, q2)])
    loads(4, [(skip1h, skip1), (skip2h, skip2)])
    weight_loads(5, w1h, w1)

    for home in greeters:

        @pl.when(me != home)
        def _():
            pl.semaphore_signal(barrier, inc=1, device_id=(home // minor, home % minor), device_id_type=MESH)

    weight_loads(6, w2h, w2)

    def cols(c):
        return slice(c * WIDE, (c + 1) * WIDE)

    def border(c):
        return pltpu.make_async_remote_copy(
            src_ref=win.at[c, pl.ds(rows, rows), :], dst_ref=win.at[c, pl.ds(0, rows), :],
            send_sem=sent.at[0], recv_sem=brecv.at[min(c // 2, chunks - 1) + (1 if c == pieces - 1 else 0)],
            device_id=place(lax.rem(me + 1, n)), device_id_type=MESH,
        )

    def thin(p):
        return slice(p * NARROW, (p + 1) * NARROW)

    early = jnp.logical_and(jnp.logical_not(greeter), me < n - 1)
    loaded(0, kv)
    for c in range(chunks):
        for p in (2 * c, 2 * c + 1):
            win[p, rows:, :] = (k1[:, thin(p)].astype(f32) * v1[:, thin(p)].astype(f32)).astype(bf16)

        @pl.when(early)
        def _():
            if c == 0:
                pl.semaphore_wait(barrier, 1)
            border(2 * c).start()
            border(2 * c + 1).start()

    @pl.when(me == 0)
    def _():
        for p in range(pieces):
            win[p, :rows, :] = jnp.zeros((rows, NARROW), bf16)

    loaded(1, rates)
    index = lax.broadcasted_iota(jnp.int32, (NODES, LANES), 0)
    place_of = functools.reduce(lambda x, k: jnp.where(index == k, float(nodes[k]), x), range(NODES), jnp.zeros((NODES, LANES), f32))

    @pl.loop(0, channels // LANES)
    def _(b):
        lane = pl.ds(pl.multiple_of(b * LANES, LANES), LANES)
        lam = rate[:, lane]
        weight = res[:, lane] * jnp.sqrt(lam)
        for k in range(NODES):
            by_node[k, :, lane] = jnp.exp(lam * (-float(nodes[k])))
        total = jnp.zeros((NODES, LANES), f32)
        for r in range(modes):
            value = jnp.exp(-(jnp.broadcast_to(lam[r : r + 1], (NODES, LANES)) * place_of))
            by_mode[r, :, lane] = value
            total = total + value * jnp.broadcast_to(weight[r : r + 1], (NODES, LANES))
        coef[:, lane] = total
        hop[:, lane] = jnp.exp(lam * (-float(rows)))
        scale[:, lane] = weight * jnp.exp(-lam)

    loaded(2, table)
    loaded(3, acts)
    loaded(4, skips)

    for c in range(chunks):
        for p in (2 * c, 2 * c + 1):
            h1[p] = mm(fwd[:, :rows], taps[:, thin(p)])
        h2[c] = mm(lift[...], stacked(coef[:, cols(c)]))

    @pl.when(greeter)
    def _():
        pl.semaphore_wait(barrier, n - 1)
        @pl.when(me < n - 1)
        def _():
            for p in range(pieces):
                border(p).start()

        @pl.loop(1, n // 2)
        def _(p):
            pl.semaphore_signal(ready, inc=1, device_id=place(lax.rem(me + 2 * p, n)), device_id_type=MESH)

        pl.semaphore_signal(ready, inc=1, device_id=place(me + 1), device_id_type=MESH)

    def first_act(group):
        @pl.when(me > 0)
        def _():
            part = pl.ds(group[0], len(group))
            whole = win.at[part, pl.ds(0, rows), :]
            pltpu.make_async_copy(whole, whole, brecv.at[groups.index(group)]).wait()

        acts = []
        for p in group:
            spec = spectral_product(mm(fwd[...], win[p]), h1[p])
            short = mm(inv[rows:, :], spec)
            own = win[p, rows:, :].astype(f32)
            acts.append((q1[:, thin(p)].astype(f32) * (short + skip1[:, thin(p)] * own)).astype(bf16))
        return jnp.concatenate(acts, axis=1)

    loaded(5, w1)
    groups = [(p, p + 1) for p in range(0, pieces - 2, 2)] + [(pieces - 2,), (pieces - 1,)]
    for group in groups[:-1]:
        act = first_act(group)
        part = mm(act, w1[group[0] * NARROW : (group[-1] + 1) * NARROW, :])
        if group[0] == 0:
            acc[...] = part
        else:
            acc[...] += part

    act = first_act(groups[-1])
    @pl.when(greeter)
    def _():
        pl.semaphore_wait(ready, owners // 2 - 1)

    @pl.when(jnp.logical_not(jnp.logical_or(owner, odd)))
    def _():
        pl.semaphore_wait(ready, owners // 2)

    @pl.when(jnp.logical_and(owner, odd))
    def _():
        pl.semaphore_wait(ready, 1)

    per_chunk = WIDE // LANES
    for c in range(chunks):
        v = acc[:, cols(c)] + mm(act, w1[thin(pieces - 1), cols(c)])
        g2[c] = (k2[:, cols(c)].astype(f32) * v.astype(bf16).astype(f32)).astype(bf16)
    for c in range(chunks):
        moment = mm(mom[...], g2[c])
        coef[:, cols(c)] = moment[:NODES] + moment[NODES:]
    mate_copy = pltpu.make_async_remote_copy(
        src_ref=ends, dst_ref=mate, send_sem=sent.at[0], recv_sem=mrecv.at[0],
        device_id=place(me + 1 - 2 * lax.rem(me, 2)), device_id_type=MESH,
    )

    def end_states(combine):
        for c in range(chunks):
            e = jnp.zeros((modes, WIDE), f32)
            for k in range(NODES):
                e = e + by_node[k, :, cols(c)] * jnp.broadcast_to(coef[k : k + 1, cols(c)], (modes, WIDE))
            for i in range(per_chunk):
                o, s = divmod(c * per_chunk + i, tiles)
                part = slice(s * modes, (s + 1) * modes)
                own = e[:, i * LANES : (i + 1) * LANES]
                ends[o, part, :] = own.astype(bf16)
                if combine:
                    block = slice((c * per_chunk + i) * LANES, (c * per_chunk + i + 1) * LANES)
                    both[o, part, :] = (hop[:, block] * own + mate[o, part, :].astype(f32)).astype(bf16)

    def ends_copy(j):
        return pltpu.make_async_remote_copy(
            src_ref=both.at[j], dst_ref=got.at[lax.div(me, 2)], send_sem=sent.at[0], recv_sem=erecv.at[lax.div(me, minor)],
            device_id=(homes[j] // minor, homes[j] % minor), device_id_type=MESH,
        )

    @pl.when(odd)
    def _():
        end_states(False)
        mate_copy.start()

    @pl.when(jnp.logical_not(odd))
    def _():
        mate_copy.wait_recv()
        end_states(True)

        @pl.when(me < n - 2)
        def _():
            for j in range(owners):

                @pl.when(me != homes[j])
                def _():
                    ends_copy(j).start()

        mate_copy.start()

    def state_copy(d):
        return pltpu.make_async_remote_copy(
            src_ref=sout.at[lax.div(d, 2)], dst_ref=sin.at[mine], send_sem=sent.at[0], recv_sem=srecv.at[0],
            device_id=place(d), device_id_type=MESH,
        )

    def scan_and_serve():
        @pl.when(jnp.logical_not(odd))
        def _():
            got[lax.div(me, 2)] = both[mine]

        decays, scales = [], []
        for s in range(tiles):
            lane = pl.ds(pl.multiple_of((mine * tiles + s) * LANES, LANES), LANES)
            decays.append(hop[:, lane])
            scales.append(scale[:, lane])
        decay, weight = jnp.concatenate(decays, axis=0), jnp.concatenate(scales, axis=0)
        decay = decay * decay

        chips = minor // 2
        my_chip = lax.div(me, 2)

        def column_in(column, count):
            some = got.at[pl.ds(column * chips, count)]
            pltpu.make_async_copy(some, some, erecv.at[column]).wait()

        def serve(chip, state):
            column = lax.div(chip, chips)
            begins = lax.rem(chip, chips) == 0
            full = column < n // minor - 1
            here = jnp.logical_and(jnp.logical_and(column == lax.div(my_chip, chips), my_chip < n // 2 - 1), jnp.logical_not(odd))
            for last in range(2):
                for own in range(2):
                    ends_here = jnp.logical_and(full == (last == 0), here == (own == 1))

                    @pl.when(jnp.logical_and(begins, ends_here))
                    def _():
                        column_in(column, chips - last - own)

            state = state * decay + got[chip].astype(f32)
            sout[chip + 1] = (state * weight).astype(bf16)

            @pl.when(2 * chip + 3 != me)
            def _():
                state_copy(2 * chip + 3).start()

            @pl.when(2 * chip + 3 == me)
            def _():
                sin[mine] = sout[chip + 1]

            @pl.when(2 * chip + 2 != me)
            def _():
                state_copy(2 * chip + 2).start()

            @pl.when(2 * chip + 2 == me)
            def _():
                sin[mine] = sout[chip + 1]

            return state

        lax.fori_loop(0, n // 2 - 1, serve, jnp.zeros((tiles * modes, LANES), f32))

    pl.when(jnp.logical_and(owner, me >= 2))(scan_and_serve)

    for c in range(chunks):
        gated = g2[c]
        spec = spectral_product(mm(fwd[:, :rows], gated), h2[c])
        y[c] = mm(inv[:rows, :], spec) + skip2[:, cols(c)] * gated.astype(f32)

    @pl.when(me < 2)
    def _():
        sin[...] = jnp.zeros_like(sin)

    def states_in(count):
        some = sin.at[pl.ds(0, count)]
        pltpu.make_async_copy(some, some, srecv.at[0]).wait()

    @pl.when(jnp.logical_and(me >= 2, owner))
    def _():
        states_in(owners - 1)

    @pl.when(jnp.logical_and(me >= 2, jnp.logical_not(owner)))
    def _():
        states_in(owners)

    @pl.when(odd)
    def _():
        mate_copy.wait_recv()

    for b in range(chunks * per_chunk):
        o, s = divmod(b, tiles)
        lane, part = slice(b * LANES, (b + 1) * LANES), slice(s * modes, (s + 1) * modes)
        before = sin[o, part, :].astype(f32)
        after = before * hop[:, lane] + scale[:, lane] * mate[o, part, :].astype(f32)
        start[:, lane] = jnp.where(odd, after, before)

    loaded(6, w2)
    for c in range(chunks):
        total = jnp.zeros((NODES, WIDE), f32)
        for r in range(modes):
            total = total + by_mode[r, :, cols(c)] * jnp.broadcast_to(start[r : r + 1, cols(c)], (NODES, WIDE))
        coef[:, cols(c)] = total
    for c in range(chunks):
        long = y[c] + mm(expand[...], stacked(coef[:, cols(c)]))
        g2[c] = (q2[:, cols(c)].astype(f32) * long).astype(bf16)
    for c in range(chunks):
        part = mm(g2[c], w2[cols(c), :])
        if c == 0:
            acc[...] = part
        elif c < chunks - 1:
            acc[...] += part
        else:
            out[...] = (acc[...] + part).astype(bf16)

    pl.when(jnp.logical_and(owner, me < 2))(scan_and_serve)

    def left(whole):
        pltpu.make_async_copy(whole, whole, sent.at[0]).wait()

    @pl.when(me < n - 1)
    def _():
        left(win.at[:, pl.ds(0, rows), :])

    left(ends)
    sender = jnp.logical_and(me < n - 2, jnp.logical_not(odd))

    @pl.when(jnp.logical_and(sender, jnp.logical_not(owner)))
    def _():
        left(both)

    @pl.when(jnp.logical_and(sender, owner))
    def _():
        left(both.at[pl.ds(0, owners - 1)])

    @pl.when(owner)
    def _():
        left(sout.at[pl.ds(0, n // 2 - 2)])

        @pl.when(me < 2)
        def _():
            left(sout)

        @pl.when(me >= 2)
        def _():
            left(sout.at[pl.ds(0, n // 2 - 1)])


def store(src, dst, sem):
    part = src.shape[0] // sem.shape[0]
    copies = [
        pltpu.make_async_copy(src.at[pl.ds(i * part, part)], dst.at[pl.ds(i * part, part)], sem.at[i])
        for i in range(sem.shape[0])
    ]
    for copy in copies:
        copy.start()
    for copy in copies:
        copy.wait()


def local(q1, k1, v1, taps, skip1, w1, q2, k2, residue, rate, skip2, w2):
    rows, channels = q1.shape
    modes = rate.shape[0]
    minor = lax.axis_size("seqmin")
    n = lax.axis_size("seqmaj") * minor
    table, nodes = tables(rows)
    operands = (q1, k1, v1, taps, skip1[None], w1, q2, k2, residue, rate, skip2[None], w2, table)
    operands = [pltpu.with_memory_space_constraint(a, pltpu.HBM) for a in operands]
    chunks, pieces, tiles = channels // WIDE, channels // NARROW, channels // (LANES * OWNERS)
    scratch = [
        pltpu.VMEM((2, rows, channels), bf16),
        pltpu.VMEM((2, modes, channels), f32),
        pltpu.VMEM(table.shape, bf16),
        pltpu.VMEM((4, rows, channels), bf16),
        pltpu.VMEM((2, 1, channels), f32),
        pltpu.VMEM(w1.shape, bf16),
        pltpu.VMEM(w2.shape, bf16),
        pltpu.VMEM((pieces, 2 * rows, NARROW), bf16),
        pltpu.VMEM((pieces, 2 * rows, NARROW), f32),
        pltpu.VMEM((chunks, 2 * rows, WIDE), f32),
        pltpu.VMEM((NODES, modes, channels), f32),
        pltpu.VMEM((modes, NODES, channels), f32),
        pltpu.VMEM((NODES, channels), f32),
        pltpu.VMEM((modes, channels), f32),
        pltpu.VMEM((modes, channels), f32),
        pltpu.VMEM((modes, channels), f32),
        pltpu.VMEM((rows, channels), f32),
        pltpu.VMEM((chunks, rows, WIDE), f32),
        pltpu.VMEM((chunks, rows, WIDE), bf16),
        pltpu.VMEM((OWNERS, tiles * modes, LANES), bf16),
        pltpu.VMEM((OWNERS, tiles * modes, LANES), bf16),
        pltpu.VMEM((OWNERS, tiles * modes, LANES), bf16),
        pltpu.VMEM((n // 2, tiles * modes, LANES), bf16),
        pltpu.VMEM((n // 2, tiles * modes, LANES), bf16),
        pltpu.VMEM((OWNERS, tiles * modes, LANES), bf16),
        pltpu.SemaphoreType.DMA((7,)),
        pltpu.SemaphoreType.DMA((chunks + 1,)),
        pltpu.SemaphoreType.DMA((n // minor,)),
        pltpu.SemaphoreType.DMA((1,)),
        pltpu.SemaphoreType.DMA((1,)),
        pltpu.SemaphoreType.DMA((1,)),
        pltpu.SemaphoreType.REGULAR,
    ]
    mixed = pl.pallas_call(
        functools.partial(kernel, n, minor, nodes),
        out_shape=pltpu.VMEM((rows, channels), bf16),
        in_specs=[pl.BlockSpec(memory_space=pltpu.HBM)] * len(operands),
        out_specs=pl.BlockSpec(memory_space=pltpu.VMEM),
        scratch_shapes=scratch,
        compiler_params=pltpu.CompilerParams(
            collective_id=0, has_side_effects=True, vmem_limit_bytes=56 * 1024 * 1024
        ),
    )(*operands)
    return pl.pallas_call(
        store,
        out_shape=jax.ShapeDtypeStruct((rows, channels), bf16),
        in_specs=[pl.BlockSpec(memory_space=pl.ANY)],
        out_specs=pl.BlockSpec(memory_space=pl.ANY),
        scratch_shapes=[pltpu.SemaphoreType.DMA((1,))],
    )(pltpu.with_memory_space_constraint(mixed, pltpu.VMEM))


def solution(mesh):
    s, r = P(axes, None), P()
    specs = (s, s, s, r, r, r, s, s, r, r, r, r)
    return jax.shard_map(local, mesh=mesh, in_specs=specs, out_specs=s, check_vma=False)
```

```python
import functools

import jax
import jax.numpy as jnp
import ml_dtypes
import numpy as np
from jax import lax
from jax.experimental import pallas as pl
from jax.experimental.pallas import tpu as pltpu
from jax.sharding import PartitionSpec as P

axes = ("seqmaj", "seqmin")
MESH = pl.DeviceIdType.MESH
f32, bf16 = jnp.float32, jnp.bfloat16
WIDE = 512
NARROW = 256
LANES = 128
NODES = 16
OWNERS = 16


def owner_places(n, minor):
    order = sorted((i, -c) for i in range(minor // 2) for c in range(n // minor))
    return [2 * i - c * minor + core for i, c in reversed(order[: OWNERS // 2]) for core in range(2)]


def split(table):
    high = table.astype(ml_dtypes.bfloat16).astype(np.float64)
    return high, table - high


def tables(rows):
    size = 2 * rows
    theta = 2.0 * np.pi * (np.arange(rows) + 0.5) / size
    angle = theta[:, None] * np.arange(size)[None, :]
    forward = np.concatenate([np.cos(angle), np.sin(angle)], axis=0)
    inverse = forward.T / rows
    nodes = 0.5 * (rows - 1) * (1.0 - np.cos(np.pi * (np.arange(NODES) + 0.5) / NODES))
    t = np.arange(rows, dtype=np.float64)
    basis = np.stack([
        np.prod([(t - nodes[m]) / (nodes[k] - nodes[m]) for m in range(NODES) if m != k], axis=0) for k in range(NODES)
    ], axis=1)
    high, low = split(basis)
    expand = np.concatenate([high, high, low], axis=1)
    moments = np.concatenate([high[::-1].T, low[::-1].T], axis=0)
    high, low = split(forward[:, :rows] @ basis)
    lift = np.concatenate([high, high, low], axis=1)
    parts = [np.pad(a, ((0, 0), (0, size - a.shape[1]))) for a in (forward, inverse, lift, expand, moments)]
    return jnp.asarray(np.concatenate(parts, axis=0), bf16), nodes


def mm(a, b):
    return jnp.dot(a, b, preferred_element_type=f32)


def spectral_product(x, h):
    half = x.shape[0] // 2
    xc, xs, hc, hs = x[:half], x[half:], h[:half], h[half:]
    return jnp.concatenate([xc * hc - xs * hs, xc * hs + xs * hc], axis=0).astype(bf16)


def stacked(x):
    high = x.astype(bf16)
    low = (x - high.astype(f32)).astype(bf16)
    return jnp.concatenate([high, low, high], axis=0)


def kernel(
    n, minor, nodes,
    q1h, k1h, v1h, tapsh, skip1h, w1h, q2h, k2h, resh, rateh, skip2h, w2h, tableh, out,
    kv, rates, table, acts, skips, w1, w2,
    win, h1, h2, by_node, by_mode, coef, hop, scale, start, acc, y, g2, ends, mate, both, got, sout, sin,
    load_sem, brecv, erecv, mrecv, srecv, sent, ready,
):
    k1, v1 = kv.at[0], kv.at[1]
    rate, res = rates.at[0], rates.at[1]
    taps, q1, k2, q2 = (acts.at[i] for i in range(4))
    skip1, skip2 = skips.at[0], skips.at[1]
    rows, channels = q1h.shape
    modes = rateh.shape[0]
    size = 2 * rows
    fwd, inv = table.at[pl.ds(0, size), :], table.at[pl.ds(size, size), :]
    lift = table.at[pl.ds(2 * size, size), pl.ds(0, 3 * NODES)]
    expand = table.at[pl.ds(3 * size, rows), pl.ds(0, 3 * NODES)]
    mom = table.at[pl.ds(3 * size + rows, 2 * NODES), pl.ds(0, rows)]
    chunks = channels // WIDE
    pieces = channels // NARROW
    owners = ends.shape[0]
    tiles = ends.shape[1] // modes
    me = lax.axis_index("seqmaj") * minor + lax.axis_index("seqmin")
    homes = owner_places(n, minor)
    mine = functools.reduce(lambda m, j: jnp.where(me == homes[j], j, m), range(owners), 0)
    owner = functools.reduce(jnp.logical_or, [me == home for home in homes])
    odd = lax.rem(me, 2) == 1
    greeter = jnp.logical_and(owner, jnp.logical_not(odd))
    greeters = homes[::2]

    def place(d):
        return (lax.div(d, minor), lax.rem(d, minor))

    barrier = pltpu.get_barrier_semaphore()

    @pl.when(me > 0)
    def _():
        @pl.when(jnp.logical_not(functools.reduce(jnp.logical_or, [me - 1 == home for home in greeters])))
        def _():
            pl.semaphore_signal(barrier, inc=1, device_id=place(me - 1), device_id_type=MESH)

    def loads(sem, copies):
        for src, dst in copies:
            pltpu.make_async_copy(src, dst, load_sem.at[sem]).start()

    def loaded(sem, whole):
        pltpu.make_async_copy(whole, whole, load_sem.at[sem]).wait()

    def weight_loads(sem, src, dst):
        spans = [pl.ds(c * WIDE, WIDE) for c in range(chunks)]
        loads(sem, [(src.at[span, :], dst.at[span, :]) for span in spans])

    loads(0, [(k1h, k1), (v1h, v1)])
    loads(1, [(rateh, rate), (resh, res)])
    loads(2, [(tableh, table)])
    loads(3, [(tapsh, taps), (q1h, q1), (k2h, k2), (q2h, q2)])
    loads(4, [(skip1h, skip1), (skip2h, skip2)])
    weight_loads(5, w1h, w1)

    for home in greeters:

        @pl.when(me != home)
        def _():
            pl.semaphore_signal(barrier, inc=1, device_id=(home // minor, home % minor), device_id_type=MESH)

    weight_loads(6, w2h, w2)

    def cols(c):
        return slice(c * WIDE, (c + 1) * WIDE)

    def border(c):
        return pltpu.make_async_remote_copy(
            src_ref=win.at[c, pl.ds(rows, rows), :], dst_ref=win.at[c, pl.ds(0, rows), :],
            send_sem=sent.at[0], recv_sem=brecv.at[min(c // 2, chunks - 1) + (1 if c == pieces - 1 else 0)],
            device_id=place(lax.rem(me + 1, n)), device_id_type=MESH,
        )

    def thin(p):
        return slice(p * NARROW, (p + 1) * NARROW)

    early = jnp.logical_and(jnp.logical_not(greeter), me < n - 1)
    loaded(0, kv)
    for c in range(chunks):
        for p in (2 * c, 2 * c + 1):
            win[p, rows:, :] = (k1[:, thin(p)].astype(f32) * v1[:, thin(p)].astype(f32)).astype(bf16)

        @pl.when(early)
        def _():
            if c == 0:
                pl.semaphore_wait(barrier, 1)
            border(2 * c).start()
            border(2 * c + 1).start()

    @pl.when(me == 0)
    def _():
        for p in range(pieces):
            win[p, :rows, :] = jnp.zeros((rows, NARROW), bf16)

    loaded(1, rates)
    index = lax.broadcasted_iota(jnp.int32, (NODES, LANES), 0)
    place_of = functools.reduce(lambda x, k: jnp.where(index == k, float(nodes[k]), x), range(NODES), jnp.zeros((NODES, LANES), f32))

    @pl.loop(0, channels // LANES)
    def _(b):
        lane = pl.ds(pl.multiple_of(b * LANES, LANES), LANES)
        lam = rate[:, lane]
        weight = res[:, lane] * jnp.sqrt(lam)
        for k in range(NODES):
            by_node[k, :, lane] = jnp.exp(lam * (-float(nodes[k])))
        total = jnp.zeros((NODES, LANES), f32)
        for r in range(modes):
            value = jnp.exp(-(jnp.broadcast_to(lam[r : r + 1], (NODES, LANES)) * place_of))
            by_mode[r, :, lane] = value
            total = total + value * jnp.broadcast_to(weight[r : r + 1], (NODES, LANES))
        coef[:, lane] = total
        hop[:, lane] = jnp.exp(lam * (-float(rows)))
        scale[:, lane] = weight * jnp.exp(-lam)

    loaded(2, table)
    loaded(3, acts)
    loaded(4, skips)

    for c in range(chunks):
        for p in (2 * c, 2 * c + 1):
            h1[p] = mm(fwd[:, :rows], taps[:, thin(p)])
        h2[c] = mm(lift[...], stacked(coef[:, cols(c)]))

    @pl.when(greeter)
    def _():
        pl.semaphore_wait(barrier, n - 1)
        @pl.when(me < n - 1)
        def _():
            for p in range(pieces):
                border(p).start()

        @pl.loop(1, n // 2)
        def _(p):
            pl.semaphore_signal(ready, inc=1, device_id=place(lax.rem(me + 2 * p, n)), device_id_type=MESH)

        pl.semaphore_signal(ready, inc=1, device_id=place(me + 1), device_id_type=MESH)

    def first_act(group):
        @pl.when(me > 0)
        def _():
            part = pl.ds(group[0], len(group))
            whole = win.at[part, pl.ds(0, rows), :]
            pltpu.make_async_copy(whole, whole, brecv.at[groups.index(group)]).wait()

        acts = []
        for p in group:
            spec = spectral_product(mm(fwd[...], win[p]), h1[p])
            short = mm(inv[rows:, :], spec)
            own = win[p, rows:, :].astype(f32)
            acts.append((q1[:, thin(p)].astype(f32) * (short + skip1[:, thin(p)] * own)).astype(bf16))
        return jnp.concatenate(acts, axis=1)

    loaded(5, w1)
    groups = [(p, p + 1) for p in range(0, pieces - 2, 2)] + [(pieces - 2,), (pieces - 1,)]
    for group in groups[:-1]:
        act = first_act(group)
        part = mm(act, w1[group[0] * NARROW : (group[-1] + 1) * NARROW, :])
        if group[0] == 0:
            acc[...] = part
        else:
            acc[...] += part

    act = first_act(groups[-1])
    @pl.when(greeter)
    def _():
        pl.semaphore_wait(ready, owners // 2 - 1)

    @pl.when(jnp.logical_not(jnp.logical_or(owner, odd)))
    def _():
        pl.semaphore_wait(ready, owners // 2)

    @pl.when(jnp.logical_and(owner, odd))
    def _():
        pl.semaphore_wait(ready, 1)

    per_chunk = WIDE // LANES
    for c in range(chunks):
        v = acc[:, cols(c)] + mm(act, w1[thin(pieces - 1), cols(c)])
        g2[c] = (k2[:, cols(c)].astype(f32) * v.astype(bf16).astype(f32)).astype(bf16)
    for c in range(chunks):
        moment = mm(mom[...], g2[c])
        coef[:, cols(c)] = moment[:NODES] + moment[NODES:]
    for c in range(chunks):
        e = jnp.zeros((modes, WIDE), f32)
        for k in range(NODES):
            e = e + by_node[k, :, cols(c)] * jnp.broadcast_to(coef[k : k + 1, cols(c)], (modes, WIDE))
        for i in range(per_chunk):
            o, s = divmod(c * per_chunk + i, tiles)
            ends[o, s * modes : (s + 1) * modes, :] = e[:, i * LANES : (i + 1) * LANES].astype(bf16)

    def ends_copy(j):
        return pltpu.make_async_remote_copy(
            src_ref=both.at[j], dst_ref=got.at[lax.div(me, 2)], send_sem=sent.at[0], recv_sem=erecv.at[lax.div(me, minor)],
            device_id=(homes[j] // minor, homes[j] % minor), device_id_type=MESH,
        )

    mate_copy = pltpu.make_async_remote_copy(
        src_ref=ends, dst_ref=mate, send_sem=sent.at[0], recv_sem=mrecv.at[0],
        device_id=place(me + 1 - 2 * lax.rem(me, 2)), device_id_type=MESH,
    )
    mate_copy.start()

    @pl.when(jnp.logical_not(odd))
    def _():
        mate_copy.wait_recv()
        for b in range(chunks * per_chunk):
            o, s = divmod(b, tiles)
            part = slice(s * modes, (s + 1) * modes)
            carried = hop[:, b * LANES : (b + 1) * LANES] * ends[o, part, :].astype(f32)
            both[o, part, :] = (carried + mate[o, part, :].astype(f32)).astype(bf16)

        @pl.when(me < n - 2)
        def _():
            for j in range(owners):

                @pl.when(me != homes[j])
                def _():
                    ends_copy(j).start()

    def state_copy(d):
        return pltpu.make_async_remote_copy(
            src_ref=sout.at[lax.div(d, 2)], dst_ref=sin.at[mine], send_sem=sent.at[0], recv_sem=srecv.at[0],
            device_id=place(d), device_id_type=MESH,
        )

    def scan_and_serve():
        @pl.when(jnp.logical_not(odd))
        def _():
            got[lax.div(me, 2)] = both[mine]

        decays, scales = [], []
        for s in range(tiles):
            lane = pl.ds(pl.multiple_of((mine * tiles + s) * LANES, LANES), LANES)
            decays.append(hop[:, lane])
            scales.append(scale[:, lane])
        decay, weight = jnp.concatenate(decays, axis=0), jnp.concatenate(scales, axis=0)
        decay = decay * decay

        chips = minor // 2
        my_chip = lax.div(me, 2)

        def column_in(column, count):
            some = got.at[pl.ds(column * chips, count)]
            pltpu.make_async_copy(some, some, erecv.at[column]).wait()

        def serve(chip, state):
            column = lax.div(chip, chips)
            begins = lax.rem(chip, chips) == 0
            full = column < n // minor - 1
            here = jnp.logical_and(jnp.logical_and(column == lax.div(my_chip, chips), my_chip < n // 2 - 1), jnp.logical_not(odd))
            for last in range(2):
                for own in range(2):
                    ends_here = jnp.logical_and(full == (last == 0), here == (own == 1))

                    @pl.when(jnp.logical_and(begins, ends_here))
                    def _():
                        column_in(column, chips - last - own)

            state = state * decay + got[chip].astype(f32)
            sout[chip + 1] = (state * weight).astype(bf16)

            @pl.when(2 * chip + 3 != me)
            def _():
                state_copy(2 * chip + 3).start()

            @pl.when(2 * chip + 3 == me)
            def _():
                sin[mine] = sout[chip + 1]

            @pl.when(2 * chip + 2 != me)
            def _():
                state_copy(2 * chip + 2).start()

            @pl.when(2 * chip + 2 == me)
            def _():
                sin[mine] = sout[chip + 1]

            return state

        lax.fori_loop(0, n // 2 - 1, serve, jnp.zeros((tiles * modes, LANES), f32))

    pl.when(jnp.logical_and(owner, me >= 2))(scan_and_serve)

    for c in range(chunks):
        gated = g2[c]
        spec = spectral_product(mm(fwd[:, :rows], gated), h2[c])
        y[c] = mm(inv[:rows, :], spec) + skip2[:, cols(c)] * gated.astype(f32)

    @pl.when(me < 2)
    def _():
        sin[...] = jnp.zeros_like(sin)

    def states_in(count):
        some = sin.at[pl.ds(0, count)]
        pltpu.make_async_copy(some, some, srecv.at[0]).wait()

    @pl.when(jnp.logical_and(me >= 2, owner))
    def _():
        states_in(owners - 1)

    @pl.when(jnp.logical_and(me >= 2, jnp.logical_not(owner)))
    def _():
        states_in(owners)

    @pl.when(odd)
    def _():
        mate_copy.wait_recv()

    for b in range(chunks * per_chunk):
        o, s = divmod(b, tiles)
        lane, part = slice(b * LANES, (b + 1) * LANES), slice(s * modes, (s + 1) * modes)
        before = sin[o, part, :].astype(f32)
        after = before * hop[:, lane] + scale[:, lane] * mate[o, part, :].astype(f32)
        start[:, lane] = jnp.where(odd, after, before)

    loaded(6, w2)
    for c in range(chunks):
        total = jnp.zeros((NODES, WIDE), f32)
        for r in range(modes):
            total = total + by_mode[r, :, cols(c)] * jnp.broadcast_to(start[r : r + 1, cols(c)], (NODES, WIDE))
        coef[:, cols(c)] = total
    for c in range(chunks):
        long = y[c] + mm(expand[...], stacked(coef[:, cols(c)]))
        g2[c] = (q2[:, cols(c)].astype(f32) * long).astype(bf16)
    for c in range(chunks):
        part = mm(g2[c], w2[cols(c), :])
        if c == 0:
            acc[...] = part
        elif c < chunks - 1:
            acc[...] += part
        else:
            out[...] = (acc[...] + part).astype(bf16)

    pl.when(jnp.logical_and(owner, me < 2))(scan_and_serve)

    def left(whole):
        pltpu.make_async_copy(whole, whole, sent.at[0]).wait()

    @pl.when(me < n - 1)
    def _():
        left(win.at[:, pl.ds(0, rows), :])

    left(ends)
    sender = jnp.logical_and(me < n - 2, jnp.logical_not(odd))

    @pl.when(jnp.logical_and(sender, jnp.logical_not(owner)))
    def _():
        left(both)

    @pl.when(jnp.logical_and(sender, owner))
    def _():
        left(both.at[pl.ds(0, owners - 1)])

    @pl.when(owner)
    def _():
        left(sout.at[pl.ds(0, n // 2 - 2)])

        @pl.when(me < 2)
        def _():
            left(sout)

        @pl.when(me >= 2)
        def _():
            left(sout.at[pl.ds(0, n // 2 - 1)])


def store(src, dst, sem):
    part = src.shape[0] // sem.shape[0]
    copies = [
        pltpu.make_async_copy(src.at[pl.ds(i * part, part)], dst.at[pl.ds(i * part, part)], sem.at[i])
        for i in range(sem.shape[0])
    ]
    for copy in copies:
        copy.start()
    for copy in copies:
        copy.wait()


def local(q1, k1, v1, taps, skip1, w1, q2, k2, residue, rate, skip2, w2):
    rows, channels = q1.shape
    modes = rate.shape[0]
    minor = lax.axis_size("seqmin")
    n = lax.axis_size("seqmaj") * minor
    table, nodes = tables(rows)
    operands = (q1, k1, v1, taps, skip1[None], w1, q2, k2, residue, rate, skip2[None], w2, table)
    operands = [pltpu.with_memory_space_constraint(a, pltpu.HBM) for a in operands]
    chunks, pieces, tiles = channels // WIDE, channels // NARROW, channels // (LANES * OWNERS)
    scratch = [
        pltpu.VMEM((2, rows, channels), bf16),
        pltpu.VMEM((2, modes, channels), f32),
        pltpu.VMEM(table.shape, bf16),
        pltpu.VMEM((4, rows, channels), bf16),
        pltpu.VMEM((2, 1, channels), f32),
        pltpu.VMEM(w1.shape, bf16),
        pltpu.VMEM(w2.shape, bf16),
        pltpu.VMEM((pieces, 2 * rows, NARROW), bf16),
        pltpu.VMEM((pieces, 2 * rows, NARROW), f32),
        pltpu.VMEM((chunks, 2 * rows, WIDE), f32),
        pltpu.VMEM((NODES, modes, channels), f32),
        pltpu.VMEM((modes, NODES, channels), f32),
        pltpu.VMEM((NODES, channels), f32),
        pltpu.VMEM((modes, channels), f32),
        pltpu.VMEM((modes, channels), f32),
        pltpu.VMEM((modes, channels), f32),
        pltpu.VMEM((rows, channels), f32),
        pltpu.VMEM((chunks, rows, WIDE), f32),
        pltpu.VMEM((chunks, rows, WIDE), bf16),
        pltpu.VMEM((OWNERS, tiles * modes, LANES), bf16),
        pltpu.VMEM((OWNERS, tiles * modes, LANES), bf16),
        pltpu.VMEM((OWNERS, tiles * modes, LANES), bf16),
        pltpu.VMEM((n // 2, tiles * modes, LANES), bf16),
        pltpu.VMEM((n // 2, tiles * modes, LANES), bf16),
        pltpu.VMEM((OWNERS, tiles * modes, LANES), bf16),
        pltpu.SemaphoreType.DMA((7,)),
        pltpu.SemaphoreType.DMA((chunks + 1,)),
        pltpu.SemaphoreType.DMA((n // minor,)),
        pltpu.SemaphoreType.DMA((1,)),
        pltpu.SemaphoreType.DMA((1,)),
        pltpu.SemaphoreType.DMA((1,)),
        pltpu.SemaphoreType.REGULAR,
    ]
    mixed = pl.pallas_call(
        functools.partial(kernel, n, minor, nodes),
        out_shape=pltpu.VMEM((rows, channels), bf16),
        in_specs=[pl.BlockSpec(memory_space=pltpu.HBM)] * len(operands),
        out_specs=pl.BlockSpec(memory_space=pltpu.VMEM),
        scratch_shapes=scratch,
        compiler_params=pltpu.CompilerParams(
            collective_id=0, has_side_effects=True, vmem_limit_bytes=56 * 1024 * 1024
        ),
    )(*operands)
    return pl.pallas_call(
        store,
        out_shape=jax.ShapeDtypeStruct((rows, channels), bf16),
        in_specs=[pl.BlockSpec(memory_space=pl.ANY)],
        out_specs=pl.BlockSpec(memory_space=pl.ANY),
        scratch_shapes=[pltpu.SemaphoreType.DMA((1,))],
    )(pltpu.with_memory_space_constraint(mixed, pltpu.VMEM))


def solution(mesh):
    s, r = P(axes, None), P()
    specs = (s, s, s, r, r, r, s, s, r, r, r, r)
    return jax.shard_map(local, mesh=mesh, in_specs=specs, out_specs=s, check_vma=False)
```

```python
import functools

import jax
import jax.numpy as jnp
import ml_dtypes
import numpy as np
from jax import lax
from jax.experimental import pallas as pl
from jax.experimental.pallas import tpu as pltpu
from jax.sharding import PartitionSpec as P

axes = ("seqmaj", "seqmin")
MESH = pl.DeviceIdType.MESH
f32, bf16 = jnp.float32, jnp.bfloat16
WIDE = 512
NARROW = 256
LANES = 128
NODES = 16
OWNERS = 16


def owner_places(n, minor):
    order = sorted((i, -c) for i in range(minor // 2) for c in range(n // minor))
    return [2 * i - c * minor + core for i, c in reversed(order[: OWNERS // 2]) for core in range(2)]


def split(table):
    high = table.astype(ml_dtypes.bfloat16).astype(np.float64)
    return high, table - high


def tables(rows):
    size = 2 * rows
    theta = 2.0 * np.pi * (np.arange(rows) + 0.5) / size
    angle = theta[:, None] * np.arange(size)[None, :]
    forward = np.concatenate([np.cos(angle), np.sin(angle)], axis=0)
    inverse = forward.T / rows
    nodes = 0.5 * (rows - 1) * (1.0 - np.cos(np.pi * (np.arange(NODES) + 0.5) / NODES))
    t = np.arange(rows, dtype=np.float64)
    basis = np.stack([
        np.prod([(t - nodes[m]) / (nodes[k] - nodes[m]) for m in range(NODES) if m != k], axis=0) for k in range(NODES)
    ], axis=1)
    high, low = split(basis)
    expand = np.concatenate([high, high, low], axis=1)
    moments = np.concatenate([high[::-1].T, low[::-1].T], axis=0)
    high, low = split(forward[:, :rows] @ basis)
    lift = np.concatenate([high, high, low], axis=1)
    parts = [np.pad(a, ((0, 0), (0, size - a.shape[1]))) for a in (forward, inverse, lift, expand, moments)]
    return jnp.asarray(np.concatenate(parts, axis=0), bf16), nodes


def mm(a, b):
    return jnp.dot(a, b, preferred_element_type=f32)


def spectral_product(x, h):
    half = x.shape[0] // 2
    xc, xs, hc, hs = x[:half], x[half:], h[:half], h[half:]
    return jnp.concatenate([xc * hc - xs * hs, xc * hs + xs * hc], axis=0).astype(bf16)


def stacked(x):
    high = x.astype(bf16)
    low = (x - high.astype(f32)).astype(bf16)
    return jnp.concatenate([high, low, high], axis=0)


def kernel(
    n, minor, nodes,
    q1h, k1h, v1h, tapsh, skip1h, w1h, q2h, k2h, resh, rateh, skip2h, w2h, tableh, out,
    kv, rates, table, acts, skips, w1, w2,
    win, h1, h2, by_node, by_mode, coef, hop, scale, start, acc, y, g2, ends, mate, both, got, sout, sin,
    load_sem, brecv, erecv, mrecv, srecv, sent, ready,
):
    k1, v1 = kv.at[0], kv.at[1]
    rate, res = rates.at[0], rates.at[1]
    taps, q1, k2, q2 = (acts.at[i] for i in range(4))
    skip1, skip2 = skips.at[0], skips.at[1]
    rows, channels = q1h.shape
    modes = rateh.shape[0]
    size = 2 * rows
    fwd, inv = table.at[pl.ds(0, size), :], table.at[pl.ds(size, size), :]
    lift = table.at[pl.ds(2 * size, size), pl.ds(0, 3 * NODES)]
    expand = table.at[pl.ds(3 * size, rows), pl.ds(0, 3 * NODES)]
    mom = table.at[pl.ds(3 * size + rows, 2 * NODES), pl.ds(0, rows)]
    chunks = channels // WIDE
    pieces = channels // NARROW
    owners = ends.shape[0]
    tiles = ends.shape[1] // modes
    me = lax.axis_index("seqmaj") * minor + lax.axis_index("seqmin")
    homes = owner_places(n, minor)
    mine = functools.reduce(lambda m, j: jnp.where(me == homes[j], j, m), range(owners), 0)
    owner = functools.reduce(jnp.logical_or, [me == home for home in homes])
    odd = lax.rem(me, 2) == 1
    greeter = jnp.logical_and(owner, jnp.logical_not(odd))
    greeters = homes[::2]

    def place(d):
        return (lax.div(d, minor), lax.rem(d, minor))

    barrier = pltpu.get_barrier_semaphore()

    @pl.when(me > 0)
    def _():
        @pl.when(jnp.logical_not(functools.reduce(jnp.logical_or, [me - 1 == home for home in greeters])))
        def _():
            pl.semaphore_signal(barrier, inc=1, device_id=place(me - 1), device_id_type=MESH)

    def loads(sem, copies):
        for src, dst in copies:
            pltpu.make_async_copy(src, dst, load_sem.at[sem]).start()

    def loaded(sem, whole):
        pltpu.make_async_copy(whole, whole, load_sem.at[sem]).wait()

    def weight_loads(sem, src, dst):
        spans = [pl.ds(c * WIDE, WIDE) for c in range(chunks)]
        loads(sem, [(src.at[span, :], dst.at[span, :]) for span in spans])

    loads(0, [(k1h, k1), (v1h, v1)])
    loads(1, [(rateh, rate), (resh, res)])
    loads(2, [(tableh, table)])
    loads(3, [(tapsh, taps), (q1h, q1), (k2h, k2), (q2h, q2)])
    loads(4, [(skip1h, skip1), (skip2h, skip2)])
    weight_loads(5, w1h, w1)

    for home in greeters:

        @pl.when(me != home)
        def _():
            pl.semaphore_signal(barrier, inc=1, device_id=(home // minor, home % minor), device_id_type=MESH)

    weight_loads(6, w2h, w2)

    def cols(c):
        return slice(c * WIDE, (c + 1) * WIDE)

    def border(c):
        return pltpu.make_async_remote_copy(
            src_ref=win.at[c, pl.ds(rows, rows), :], dst_ref=win.at[c, pl.ds(0, rows), :],
            send_sem=sent.at[0], recv_sem=brecv.at[min(c // 2, chunks - 1) + (1 if c == pieces - 1 else 0)],
            device_id=place(lax.rem(me + 1, n)), device_id_type=MESH,
        )

    def thin(p):
        return slice(p * NARROW, (p + 1) * NARROW)

    early = jnp.logical_and(jnp.logical_not(greeter), me < n - 1)
    loaded(0, kv)
    for c in range(chunks):
        for p in (2 * c, 2 * c + 1):
            win[p, rows:, :] = (k1[:, thin(p)].astype(f32) * v1[:, thin(p)].astype(f32)).astype(bf16)

        @pl.when(early)
        def _():
            if c == 0:
                pl.semaphore_wait(barrier, 1)
            border(2 * c).start()
            border(2 * c + 1).start()

    @pl.when(me == 0)
    def _():
        for p in range(pieces):
            win[p, :rows, :] = jnp.zeros((rows, NARROW), bf16)

    loaded(1, rates)
    index = lax.broadcasted_iota(jnp.int32, (NODES, LANES), 0)
    place_of = functools.reduce(lambda x, k: jnp.where(index == k, float(nodes[k]), x), range(NODES), jnp.zeros((NODES, LANES), f32))

    @pl.loop(0, channels // LANES)
    def _(b):
        lane = pl.ds(pl.multiple_of(b * LANES, LANES), LANES)
        lam = rate[:, lane]
        weight = res[:, lane] * jnp.sqrt(lam)
        for k in range(NODES):
            by_node[k, :, lane] = jnp.exp(lam * (-float(nodes[k])))
        total = jnp.zeros((NODES, LANES), f32)
        for r in range(modes):
            value = jnp.exp(-(jnp.broadcast_to(lam[r : r + 1], (NODES, LANES)) * place_of))
            by_mode[r, :, lane] = value
            total = total + value * jnp.broadcast_to(weight[r : r + 1], (NODES, LANES))
        coef[:, lane] = total
        hop[:, lane] = jnp.exp(lam * (-float(rows)))
        scale[:, lane] = weight * jnp.exp(-lam)

    loaded(2, table)
    loaded(3, acts)
    loaded(4, skips)

    for c in range(chunks):
        for p in (2 * c, 2 * c + 1):
            h1[p] = mm(fwd[:, :rows], taps[:, thin(p)])
        h2[c] = mm(lift[...], stacked(coef[:, cols(c)]))

    @pl.when(greeter)
    def _():
        pl.semaphore_wait(barrier, n - 1)
        @pl.when(me < n - 1)
        def _():
            for p in range(pieces):
                border(p).start()

        @pl.loop(1, n // 2)
        def _(p):
            pl.semaphore_signal(ready, inc=1, device_id=place(lax.rem(me + 2 * p, n)), device_id_type=MESH)

        pl.semaphore_signal(ready, inc=1, device_id=place(me + 1), device_id_type=MESH)

    def first_act(group):
        @pl.when(me > 0)
        def _():
            part = pl.ds(group[0], len(group))
            whole = win.at[part, pl.ds(0, rows), :]
            pltpu.make_async_copy(whole, whole, brecv.at[groups.index(group)]).wait()

        acts = []
        for p in group:
            spec = spectral_product(mm(fwd[...], win[p]), h1[p])
            short = mm(inv[rows:, :], spec)
            own = win[p, rows:, :].astype(f32)
            acts.append((q1[:, thin(p)].astype(f32) * (short + skip1[:, thin(p)] * own)).astype(bf16))
        return jnp.concatenate(acts, axis=1)

    loaded(5, w1)
    groups = [(p, p + 1) for p in range(0, pieces - 2, 2)] + [(pieces - 2,), (pieces - 1,)]
    for group in groups[:-2]:
        act = first_act(group)
        part = mm(act, w1[group[0] * NARROW : (group[-1] + 1) * NARROW, :])
        if group[0] == 0:
            acc[...] = part
        else:
            acc[...] += part

    act = jnp.concatenate([first_act(group) for group in groups[-2:]], axis=1)
    @pl.when(greeter)
    def _():
        pl.semaphore_wait(ready, owners // 2 - 1)

    @pl.when(jnp.logical_not(jnp.logical_or(owner, odd)))
    def _():
        pl.semaphore_wait(ready, owners // 2)

    @pl.when(jnp.logical_and(owner, odd))
    def _():
        pl.semaphore_wait(ready, 1)

    per_chunk = WIDE // LANES
    for c in range(chunks):
        v = acc[:, cols(c)] + mm(act, w1[channels - 2 * NARROW :, cols(c)])
        g2[c] = (k2[:, cols(c)].astype(f32) * v.astype(bf16).astype(f32)).astype(bf16)
    for c in range(chunks):
        moment = mm(mom[...], g2[c])
        coef[:, cols(c)] = moment[:NODES] + moment[NODES:]
    for c in range(chunks):
        e = jnp.zeros((modes, WIDE), f32)
        for k in range(NODES):
            e = e + by_node[k, :, cols(c)] * jnp.broadcast_to(coef[k : k + 1, cols(c)], (modes, WIDE))
        for i in range(per_chunk):
            o, s = divmod(c * per_chunk + i, tiles)
            ends[o, s * modes : (s + 1) * modes, :] = e[:, i * LANES : (i + 1) * LANES].astype(bf16)

    def ends_copy(j):
        return pltpu.make_async_remote_copy(
            src_ref=both.at[j], dst_ref=got.at[lax.div(me, 2)], send_sem=sent.at[0], recv_sem=erecv.at[lax.div(me, minor)],
            device_id=(homes[j] // minor, homes[j] % minor), device_id_type=MESH,
        )

    mate_copy = pltpu.make_async_remote_copy(
        src_ref=ends, dst_ref=mate, send_sem=sent.at[0], recv_sem=mrecv.at[0],
        device_id=place(me + 1 - 2 * lax.rem(me, 2)), device_id_type=MESH,
    )
    mate_copy.start()

    @pl.when(jnp.logical_not(odd))
    def _():
        mate_copy.wait_recv()
        for b in range(chunks * per_chunk):
            o, s = divmod(b, tiles)
            part = slice(s * modes, (s + 1) * modes)
            carried = hop[:, b * LANES : (b + 1) * LANES] * ends[o, part, :].astype(f32)
            both[o, part, :] = (carried + mate[o, part, :].astype(f32)).astype(bf16)

        @pl.when(me < n - 2)
        def _():
            for j in range(owners):

                @pl.when(me != homes[j])
                def _():
                    ends_copy(j).start()

    def state_copy(d):
        return pltpu.make_async_remote_copy(
            src_ref=sout.at[lax.div(d, 2)], dst_ref=sin.at[mine], send_sem=sent.at[0], recv_sem=srecv.at[0],
            device_id=place(d), device_id_type=MESH,
        )

    def scan_and_serve():
        @pl.when(jnp.logical_not(odd))
        def _():
            got[lax.div(me, 2)] = both[mine]

        decays, scales = [], []
        for s in range(tiles):
            lane = pl.ds(pl.multiple_of((mine * tiles + s) * LANES, LANES), LANES)
            decays.append(hop[:, lane])
            scales.append(scale[:, lane])
        decay, weight = jnp.concatenate(decays, axis=0), jnp.concatenate(scales, axis=0)
        decay = decay * decay

        chips = minor // 2
        my_chip = lax.div(me, 2)

        def column_in(column, count):
            some = got.at[pl.ds(column * chips, count)]
            pltpu.make_async_copy(some, some, erecv.at[column]).wait()

        def serve(chip, state):
            column = lax.div(chip, chips)
            begins = lax.rem(chip, chips) == 0
            full = column < n // minor - 1
            here = jnp.logical_and(jnp.logical_and(column == lax.div(my_chip, chips), my_chip < n // 2 - 1), jnp.logical_not(odd))
            for last in range(2):
                for own in range(2):
                    ends_here = jnp.logical_and(full == (last == 0), here == (own == 1))

                    @pl.when(jnp.logical_and(begins, ends_here))
                    def _():
                        column_in(column, chips - last - own)

            state = state * decay + got[chip].astype(f32)
            sout[chip + 1] = (state * weight).astype(bf16)

            @pl.when(2 * chip + 3 != me)
            def _():
                state_copy(2 * chip + 3).start()

            @pl.when(2 * chip + 3 == me)
            def _():
                sin[mine] = sout[chip + 1]

            @pl.when(2 * chip + 2 != me)
            def _():
                state_copy(2 * chip + 2).start()

            @pl.when(2 * chip + 2 == me)
            def _():
                sin[mine] = sout[chip + 1]

            return state

        lax.fori_loop(0, n // 2 - 1, serve, jnp.zeros((tiles * modes, LANES), f32))

    pl.when(jnp.logical_and(owner, me >= 2))(scan_and_serve)

    for c in range(chunks):
        gated = g2[c]
        spec = spectral_product(mm(fwd[:, :rows], gated), h2[c])
        y[c] = mm(inv[:rows, :], spec) + skip2[:, cols(c)] * gated.astype(f32)

    @pl.when(me < 2)
    def _():
        sin[...] = jnp.zeros_like(sin)

    def states_in(count):
        some = sin.at[pl.ds(0, count)]
        pltpu.make_async_copy(some, some, srecv.at[0]).wait()

    @pl.when(jnp.logical_and(me >= 2, owner))
    def _():
        states_in(owners - 1)

    @pl.when(jnp.logical_and(me >= 2, jnp.logical_not(owner)))
    def _():
        states_in(owners)

    @pl.when(odd)
    def _():
        mate_copy.wait_recv()

    for b in range(chunks * per_chunk):
        o, s = divmod(b, tiles)
        lane, part = slice(b * LANES, (b + 1) * LANES), slice(s * modes, (s + 1) * modes)
        before = sin[o, part, :].astype(f32)
        after = before * hop[:, lane] + scale[:, lane] * mate[o, part, :].astype(f32)
        start[:, lane] = jnp.where(odd, after, before)

    loaded(6, w2)
    for c in range(chunks):
        total = jnp.zeros((NODES, WIDE), f32)
        for r in range(modes):
            total = total + by_mode[r, :, cols(c)] * jnp.broadcast_to(start[r : r + 1, cols(c)], (NODES, WIDE))
        coef[:, cols(c)] = total
    for c in range(chunks):
        long = y[c] + mm(expand[...], stacked(coef[:, cols(c)]))
        g2[c] = (q2[:, cols(c)].astype(f32) * long).astype(bf16)
    for c in range(chunks):
        part = mm(g2[c], w2[cols(c), :])
        if c == 0:
            acc[...] = part
        elif c < chunks - 1:
            acc[...] += part
        else:
            out[...] = (acc[...] + part).astype(bf16)

    pl.when(jnp.logical_and(owner, me < 2))(scan_and_serve)

    def left(whole):
        pltpu.make_async_copy(whole, whole, sent.at[0]).wait()

    @pl.when(me < n - 1)
    def _():
        left(win.at[:, pl.ds(0, rows), :])

    left(ends)
    sender = jnp.logical_and(me < n - 2, jnp.logical_not(odd))

    @pl.when(jnp.logical_and(sender, jnp.logical_not(owner)))
    def _():
        left(both)

    @pl.when(jnp.logical_and(sender, owner))
    def _():
        left(both.at[pl.ds(0, owners - 1)])

    @pl.when(owner)
    def _():
        left(sout.at[pl.ds(0, n // 2 - 2)])

        @pl.when(me < 2)
        def _():
            left(sout)

        @pl.when(me >= 2)
        def _():
            left(sout.at[pl.ds(0, n // 2 - 1)])


def store(src, dst, sem):
    part = src.shape[0] // sem.shape[0]
    copies = [
        pltpu.make_async_copy(src.at[pl.ds(i * part, part)], dst.at[pl.ds(i * part, part)], sem.at[i])
        for i in range(sem.shape[0])
    ]
    for copy in copies:
        copy.start()
    for copy in copies:
        copy.wait()


def local(q1, k1, v1, taps, skip1, w1, q2, k2, residue, rate, skip2, w2):
    rows, channels = q1.shape
    modes = rate.shape[0]
    minor = lax.axis_size("seqmin")
    n = lax.axis_size("seqmaj") * minor
    table, nodes = tables(rows)
    operands = (q1, k1, v1, taps, skip1[None], w1, q2, k2, residue, rate, skip2[None], w2, table)
    operands = [pltpu.with_memory_space_constraint(a, pltpu.HBM) for a in operands]
    chunks, pieces, tiles = channels // WIDE, channels // NARROW, channels // (LANES * OWNERS)
    scratch = [
        pltpu.VMEM((2, rows, channels), bf16),
        pltpu.VMEM((2, modes, channels), f32),
        pltpu.VMEM(table.shape, bf16),
        pltpu.VMEM((4, rows, channels), bf16),
        pltpu.VMEM((2, 1, channels), f32),
        pltpu.VMEM(w1.shape, bf16),
        pltpu.VMEM(w2.shape, bf16),
        pltpu.VMEM((pieces, 2 * rows, NARROW), bf16),
        pltpu.VMEM((pieces, 2 * rows, NARROW), f32),
        pltpu.VMEM((chunks, 2 * rows, WIDE), f32),
        pltpu.VMEM((NODES, modes, channels), f32),
        pltpu.VMEM((modes, NODES, channels), f32),
        pltpu.VMEM((NODES, channels), f32),
        pltpu.VMEM((modes, channels), f32),
        pltpu.VMEM((modes, channels), f32),
        pltpu.VMEM((modes, channels), f32),
        pltpu.VMEM((rows, channels), f32),
        pltpu.VMEM((chunks, rows, WIDE), f32),
        pltpu.VMEM((chunks, rows, WIDE), bf16),
        pltpu.VMEM((OWNERS, tiles * modes, LANES), bf16),
        pltpu.VMEM((OWNERS, tiles * modes, LANES), bf16),
        pltpu.VMEM((OWNERS, tiles * modes, LANES), bf16),
        pltpu.VMEM((n // 2, tiles * modes, LANES), bf16),
        pltpu.VMEM((n // 2, tiles * modes, LANES), bf16),
        pltpu.VMEM((OWNERS, tiles * modes, LANES), bf16),
        pltpu.SemaphoreType.DMA((7,)),
        pltpu.SemaphoreType.DMA((chunks + 1,)),
        pltpu.SemaphoreType.DMA((n // minor,)),
        pltpu.SemaphoreType.DMA((1,)),
        pltpu.SemaphoreType.DMA((1,)),
        pltpu.SemaphoreType.DMA((1,)),
        pltpu.SemaphoreType.REGULAR,
    ]
    mixed = pl.pallas_call(
        functools.partial(kernel, n, minor, nodes),
        out_shape=pltpu.VMEM((rows, channels), bf16),
        in_specs=[pl.BlockSpec(memory_space=pltpu.HBM)] * len(operands),
        out_specs=pl.BlockSpec(memory_space=pltpu.VMEM),
        scratch_shapes=scratch,
        compiler_params=pltpu.CompilerParams(
            collective_id=0, has_side_effects=True, vmem_limit_bytes=56 * 1024 * 1024
        ),
    )(*operands)
    return pl.pallas_call(
        store,
        out_shape=jax.ShapeDtypeStruct((rows, channels), bf16),
        in_specs=[pl.BlockSpec(memory_space=pl.ANY)],
        out_specs=pl.BlockSpec(memory_space=pl.ANY),
        scratch_shapes=[pltpu.SemaphoreType.DMA((1,))],
    )(pltpu.with_memory_space_constraint(mixed, pltpu.VMEM))


def solution(mesh):
    s, r = P(axes, None), P()
    specs = (s, s, s, r, r, r, s, s, r, r, r, r)
    return jax.shard_map(local, mesh=mesh, in_specs=specs, out_specs=s, check_vma=False)
```

```python
import functools

import jax
import jax.numpy as jnp
import ml_dtypes
import numpy as np
from jax import lax
from jax.experimental import pallas as pl
from jax.experimental.pallas import tpu as pltpu
from jax.sharding import PartitionSpec as P

axes = ("seqmaj", "seqmin")
MESH = pl.DeviceIdType.MESH
f32, bf16 = jnp.float32, jnp.bfloat16
WIDE = 512
NARROW = 256
LANES = 128
NODES = 16
OWNERS = 16


def owner_places(n, minor):
    order = sorted((i, -c) for i in range(minor // 2) for c in range(n // minor))
    return [2 * i - c * minor + core for i, c in reversed(order[: OWNERS // 2]) for core in range(2)]


def split(table):
    high = table.astype(ml_dtypes.bfloat16).astype(np.float64)
    return high, table - high


def tables(rows):
    size = 2 * rows
    theta = 2.0 * np.pi * (np.arange(rows) + 0.5) / size
    angle = theta[:, None] * np.arange(size)[None, :]
    forward = np.concatenate([np.cos(angle), np.sin(angle)], axis=0)
    inverse = forward.T / rows
    nodes = 0.5 * (rows - 1) * (1.0 - np.cos(np.pi * (np.arange(NODES) + 0.5) / NODES))
    t = np.arange(rows, dtype=np.float64)
    basis = np.stack([
        np.prod([(t - nodes[m]) / (nodes[k] - nodes[m]) for m in range(NODES) if m != k], axis=0) for k in range(NODES)
    ], axis=1)
    high, low = split(basis)
    expand = np.concatenate([high, high, low], axis=1)
    moments = np.concatenate([high[::-1].T, low[::-1].T], axis=0)
    high, low = split(forward[:, :rows] @ basis)
    lift = np.concatenate([high, high, low], axis=1)
    parts = [np.pad(a, ((0, 0), (0, size - a.shape[1]))) for a in (forward, inverse, lift, expand, moments)]
    return jnp.asarray(np.concatenate(parts, axis=0), bf16), nodes


def mm(a, b):
    return jnp.dot(a, b, preferred_element_type=f32)


def spectral_product(x, h):
    half = x.shape[0] // 2
    xc, xs, hc, hs = x[:half], x[half:], h[:half], h[half:]
    return jnp.concatenate([xc * hc - xs * hs, xc * hs + xs * hc], axis=0).astype(bf16)


def stacked(x):
    high = x.astype(bf16)
    low = (x - high.astype(f32)).astype(bf16)
    return jnp.concatenate([high, low, high], axis=0)


def kernel(
    n, minor, nodes,
    q1h, k1h, v1h, tapsh, skip1h, w1h, q2h, k2h, resh, rateh, skip2h, w2h, tableh, out,
    kv, rates, table, acts, skips, w1, w2,
    win, h1, h2, by_node, by_mode, coef, hop, scale, start, acc, y, g2, ends, mate, both, got, sout, sin,
    load_sem, brecv, erecv, mrecv, srecv, sent, ready,
):
    k1, v1 = kv.at[0], kv.at[1]
    rate, res = rates.at[0], rates.at[1]
    taps, q1, k2, q2 = (acts.at[i] for i in range(4))
    skip1, skip2 = skips.at[0], skips.at[1]
    rows, channels = q1h.shape
    modes = rateh.shape[0]
    size = 2 * rows
    fwd, inv = table.at[pl.ds(0, size), :], table.at[pl.ds(size, size), :]
    lift = table.at[pl.ds(2 * size, size), pl.ds(0, 3 * NODES)]
    expand = table.at[pl.ds(3 * size, rows), pl.ds(0, 3 * NODES)]
    mom = table.at[pl.ds(3 * size + rows, 2 * NODES), pl.ds(0, rows)]
    chunks = channels // WIDE
    pieces = channels // NARROW
    owners = ends.shape[0]
    tiles = ends.shape[1] // modes
    me = lax.axis_index("seqmaj") * minor + lax.axis_index("seqmin")
    homes = owner_places(n, minor)
    mine = functools.reduce(lambda m, j: jnp.where(me == homes[j], j, m), range(owners), 0)
    owner = functools.reduce(jnp.logical_or, [me == home for home in homes])
    odd = lax.rem(me, 2) == 1
    greeter = jnp.logical_and(owner, jnp.logical_not(odd))
    greeters = homes[::2]

    def place(d):
        return (lax.div(d, minor), lax.rem(d, minor))

    barrier = pltpu.get_barrier_semaphore()

    @pl.when(me > 0)
    def _():
        @pl.when(jnp.logical_not(functools.reduce(jnp.logical_or, [me - 1 == home for home in greeters])))
        def _():
            pl.semaphore_signal(barrier, inc=1, device_id=place(me - 1), device_id_type=MESH)

    def loads(sem, copies):
        for src, dst in copies:
            pltpu.make_async_copy(src, dst, load_sem.at[sem]).start()

    def loaded(sem, whole):
        pltpu.make_async_copy(whole, whole, load_sem.at[sem]).wait()

    def weight_loads(sem, src, dst):
        spans = [pl.ds(c * WIDE, WIDE) for c in range(chunks)]
        loads(sem, [(src.at[span, :], dst.at[span, :]) for span in spans])

    loads(0, [(k1h, k1), (v1h, v1)])
    loads(1, [(rateh, rate), (resh, res)])
    loads(2, [(tableh, table)])
    loads(3, [(tapsh, taps), (q1h, q1), (k2h, k2), (q2h, q2)])
    loads(4, [(skip1h, skip1), (skip2h, skip2)])
    weight_loads(5, w1h, w1)

    for home in greeters:

        @pl.when(me != home)
        def _():
            pl.semaphore_signal(barrier, inc=1, device_id=(home // minor, home % minor), device_id_type=MESH)

    weight_loads(6, w2h, w2)

    def cols(c):
        return slice(c * WIDE, (c + 1) * WIDE)

    def border(c):
        return pltpu.make_async_remote_copy(
            src_ref=win.at[c, pl.ds(rows, rows), :], dst_ref=win.at[c, pl.ds(0, rows), :],
            send_sem=sent.at[0], recv_sem=brecv.at[max(c // 2, c - pieces // 2 + 2)],
            device_id=place(lax.rem(me + 1, n)), device_id_type=MESH,
        )

    def thin(p):
        return slice(p * NARROW, (p + 1) * NARROW)

    early = jnp.logical_and(jnp.logical_not(greeter), me < n - 1)
    loaded(0, kv)
    for c in range(chunks):
        for p in (2 * c, 2 * c + 1):
            win[p, rows:, :] = (k1[:, thin(p)].astype(f32) * v1[:, thin(p)].astype(f32)).astype(bf16)

        @pl.when(early)
        def _():
            if c == 0:
                pl.semaphore_wait(barrier, 1)
            border(2 * c).start()
            border(2 * c + 1).start()

    @pl.when(me == 0)
    def _():
        for p in range(pieces):
            win[p, :rows, :] = jnp.zeros((rows, NARROW), bf16)

    loaded(1, rates)
    index = lax.broadcasted_iota(jnp.int32, (NODES, LANES), 0)
    place_of = functools.reduce(lambda x, k: jnp.where(index == k, float(nodes[k]), x), range(NODES), jnp.zeros((NODES, LANES), f32))

    @pl.loop(0, channels // LANES)
    def _(b):
        lane = pl.ds(pl.multiple_of(b * LANES, LANES), LANES)
        lam = rate[:, lane]
        weight = res[:, lane] * jnp.sqrt(lam)
        for k in range(NODES):
            by_node[k, :, lane] = jnp.exp(lam * (-float(nodes[k])))
        total = jnp.zeros((NODES, LANES), f32)
        for r in range(modes):
            value = jnp.exp(-(jnp.broadcast_to(lam[r : r + 1], (NODES, LANES)) * place_of))
            by_mode[r, :, lane] = value
            total = total + value * jnp.broadcast_to(weight[r : r + 1], (NODES, LANES))
        coef[:, lane] = total
        hop[:, lane] = jnp.exp(lam * (-float(rows)))
        scale[:, lane] = weight * jnp.exp(-lam)

    loaded(2, table)
    loaded(3, acts)
    loaded(4, skips)

    for c in range(chunks):
        for p in (2 * c, 2 * c + 1):
            h1[p] = mm(fwd[:, :rows], taps[:, thin(p)])
        h2[c] = mm(lift[...], stacked(coef[:, cols(c)]))

    @pl.when(greeter)
    def _():
        pl.semaphore_wait(barrier, n - 1)
        @pl.when(me < n - 1)
        def _():
            for p in range(pieces):
                border(p).start()

        @pl.loop(1, n // 2)
        def _(p):
            pl.semaphore_signal(ready, inc=1, device_id=place(lax.rem(me + 2 * p, n)), device_id_type=MESH)

        pl.semaphore_signal(ready, inc=1, device_id=place(me + 1), device_id_type=MESH)

    def first_act(group):
        @pl.when(me > 0)
        def _():
            part = pl.ds(group[0], len(group))
            whole = win.at[part, pl.ds(0, rows), :]
            pltpu.make_async_copy(whole, whole, brecv.at[groups.index(group)]).wait()

        acts = []
        for p in group:
            spec = spectral_product(mm(fwd[...], win[p]), h1[p])
            short = mm(inv[rows:, :], spec)
            own = win[p, rows:, :].astype(f32)
            acts.append((q1[:, thin(p)].astype(f32) * (short + skip1[:, thin(p)] * own)).astype(bf16))
        return jnp.concatenate(acts, axis=1)

    loaded(5, w1)
    groups = [(p, p + 1) for p in range(0, pieces - 4, 2)] + [(p,) for p in range(pieces - 4, pieces)]
    for pair in [(group,) for group in groups[:-4]] + [tuple(groups[-4:-2])]:
        act = jnp.concatenate([first_act(group) for group in pair], axis=1)
        part = mm(act, w1[pair[0][0] * NARROW : (pair[-1][-1] + 1) * NARROW, :])
        if pair[0][0] == 0:
            acc[...] = part
        else:
            acc[...] += part

    act = jnp.concatenate([first_act(group) for group in groups[-2:]], axis=1)
    @pl.when(greeter)
    def _():
        pl.semaphore_wait(ready, owners // 2 - 1)

    @pl.when(jnp.logical_not(jnp.logical_or(owner, odd)))
    def _():
        pl.semaphore_wait(ready, owners // 2)

    @pl.when(jnp.logical_and(owner, odd))
    def _():
        pl.semaphore_wait(ready, 1)

    per_chunk = WIDE // LANES
    for c in range(chunks):
        v = acc[:, cols(c)] + mm(act, w1[channels - 2 * NARROW :, cols(c)])
        g2[c] = (k2[:, cols(c)].astype(f32) * v.astype(bf16).astype(f32)).astype(bf16)
    for c in range(chunks):
        moment = mm(mom[...], g2[c])
        coef[:, cols(c)] = moment[:NODES] + moment[NODES:]
    for c in range(chunks):
        e = jnp.zeros((modes, WIDE), f32)
        for k in range(NODES):
            e = e + by_node[k, :, cols(c)] * jnp.broadcast_to(coef[k : k + 1, cols(c)], (modes, WIDE))
        for i in range(per_chunk):
            o, s = divmod(c * per_chunk + i, tiles)
            ends[o, s * modes : (s + 1) * modes, :] = e[:, i * LANES : (i + 1) * LANES].astype(bf16)

    def ends_copy(j):
        return pltpu.make_async_remote_copy(
            src_ref=both.at[j], dst_ref=got.at[lax.div(me, 2)], send_sem=sent.at[0], recv_sem=erecv.at[lax.div(me, minor)],
            device_id=(homes[j] // minor, homes[j] % minor), device_id_type=MESH,
        )

    mate_copy = pltpu.make_async_remote_copy(
        src_ref=ends, dst_ref=mate, send_sem=sent.at[0], recv_sem=mrecv.at[0],
        device_id=place(me + 1 - 2 * lax.rem(me, 2)), device_id_type=MESH,
    )
    mate_copy.start()

    @pl.when(jnp.logical_not(odd))
    def _():
        mate_copy.wait_recv()
        for b in range(chunks * per_chunk):
            o, s = divmod(b, tiles)
            part = slice(s * modes, (s + 1) * modes)
            carried = hop[:, b * LANES : (b + 1) * LANES] * ends[o, part, :].astype(f32)
            both[o, part, :] = (carried + mate[o, part, :].astype(f32)).astype(bf16)

        @pl.when(me < n - 2)
        def _():
            for j in range(owners):

                @pl.when(me != homes[j])
                def _():
                    ends_copy(j).start()

    def state_copy(d):
        return pltpu.make_async_remote_copy(
            src_ref=sout.at[lax.div(d, 2)], dst_ref=sin.at[mine], send_sem=sent.at[0], recv_sem=srecv.at[0],
            device_id=place(d), device_id_type=MESH,
        )

    def scan_and_serve():
        @pl.when(jnp.logical_not(odd))
        def _():
            got[lax.div(me, 2)] = both[mine]

        decays, scales = [], []
        for s in range(tiles):
            lane = pl.ds(pl.multiple_of((mine * tiles + s) * LANES, LANES), LANES)
            decays.append(hop[:, lane])
            scales.append(scale[:, lane])
        decay, weight = jnp.concatenate(decays, axis=0), jnp.concatenate(scales, axis=0)
        decay = decay * decay

        chips = minor // 2
        my_chip = lax.div(me, 2)

        def column_in(column, count):
            some = got.at[pl.ds(column * chips, count)]
            pltpu.make_async_copy(some, some, erecv.at[column]).wait()

        def serve(chip, state):
            column = lax.div(chip, chips)
            begins = lax.rem(chip, chips) == 0
            full = column < n // minor - 1
            here = jnp.logical_and(jnp.logical_and(column == lax.div(my_chip, chips), my_chip < n // 2 - 1), jnp.logical_not(odd))
            for last in range(2):
                for own in range(2):
                    ends_here = jnp.logical_and(full == (last == 0), here == (own == 1))

                    @pl.when(jnp.logical_and(begins, ends_here))
                    def _():
                        column_in(column, chips - last - own)

            state = state * decay + got[chip].astype(f32)
            sout[chip + 1] = (state * weight).astype(bf16)

            @pl.when(2 * chip + 3 != me)
            def _():
                state_copy(2 * chip + 3).start()

            @pl.when(2 * chip + 3 == me)
            def _():
                sin[mine] = sout[chip + 1]

            @pl.when(2 * chip + 2 != me)
            def _():
                state_copy(2 * chip + 2).start()

            @pl.when(2 * chip + 2 == me)
            def _():
                sin[mine] = sout[chip + 1]

            return state

        lax.fori_loop(0, n // 2 - 1, serve, jnp.zeros((tiles * modes, LANES), f32))

    pl.when(jnp.logical_and(owner, me >= 2))(scan_and_serve)

    for c in range(chunks):
        gated = g2[c]
        spec = spectral_product(mm(fwd[:, :rows], gated), h2[c])
        y[c] = mm(inv[:rows, :], spec) + skip2[:, cols(c)] * gated.astype(f32)

    @pl.when(me < 2)
    def _():
        sin[...] = jnp.zeros_like(sin)

    def states_in(count):
        some = sin.at[pl.ds(0, count)]
        pltpu.make_async_copy(some, some, srecv.at[0]).wait()

    @pl.when(jnp.logical_and(me >= 2, owner))
    def _():
        states_in(owners - 1)

    @pl.when(jnp.logical_and(me >= 2, jnp.logical_not(owner)))
    def _():
        states_in(owners)

    @pl.when(odd)
    def _():
        mate_copy.wait_recv()

    for b in range(chunks * per_chunk):
        o, s = divmod(b, tiles)
        lane, part = slice(b * LANES, (b + 1) * LANES), slice(s * modes, (s + 1) * modes)
        before = sin[o, part, :].astype(f32)
        after = before * hop[:, lane] + scale[:, lane] * mate[o, part, :].astype(f32)
        start[:, lane] = jnp.where(odd, after, before)

    loaded(6, w2)
    for c in range(chunks):
        total = jnp.zeros((NODES, WIDE), f32)
        for r in range(modes):
            total = total + by_mode[r, :, cols(c)] * jnp.broadcast_to(start[r : r + 1, cols(c)], (NODES, WIDE))
        coef[:, cols(c)] = total
    for c in range(chunks):
        long = y[c] + mm(expand[...], stacked(coef[:, cols(c)]))
        g2[c] = (q2[:, cols(c)].astype(f32) * long).astype(bf16)
    for c in range(chunks):
        part = mm(g2[c], w2[cols(c), :])
        if c == 0:
            acc[...] = part
        elif c < chunks - 1:
            acc[...] += part
        else:
            out[...] = (acc[...] + part).astype(bf16)

    pl.when(jnp.logical_and(owner, me < 2))(scan_and_serve)

    def left(whole):
        pltpu.make_async_copy(whole, whole, sent.at[0]).wait()

    @pl.when(me < n - 1)
    def _():
        left(win.at[:, pl.ds(0, rows), :])

    left(ends)
    sender = jnp.logical_and(me < n - 2, jnp.logical_not(odd))

    @pl.when(jnp.logical_and(sender, jnp.logical_not(owner)))
    def _():
        left(both)

    @pl.when(jnp.logical_and(sender, owner))
    def _():
        left(both.at[pl.ds(0, owners - 1)])

    @pl.when(owner)
    def _():
        left(sout.at[pl.ds(0, n // 2 - 2)])

        @pl.when(me < 2)
        def _():
            left(sout)

        @pl.when(me >= 2)
        def _():
            left(sout.at[pl.ds(0, n // 2 - 1)])


def store(src, dst, sem):
    part = src.shape[0] // sem.shape[0]
    copies = [
        pltpu.make_async_copy(src.at[pl.ds(i * part, part)], dst.at[pl.ds(i * part, part)], sem.at[i])
        for i in range(sem.shape[0])
    ]
    for copy in copies:
        copy.start()
    for copy in copies:
        copy.wait()


def local(q1, k1, v1, taps, skip1, w1, q2, k2, residue, rate, skip2, w2):
    rows, channels = q1.shape
    modes = rate.shape[0]
    minor = lax.axis_size("seqmin")
    n = lax.axis_size("seqmaj") * minor
    table, nodes = tables(rows)
    operands = (q1, k1, v1, taps, skip1[None], w1, q2, k2, residue, rate, skip2[None], w2, table)
    operands = [pltpu.with_memory_space_constraint(a, pltpu.HBM) for a in operands]
    chunks, pieces, tiles = channels // WIDE, channels // NARROW, channels // (LANES * OWNERS)
    scratch = [
        pltpu.VMEM((2, rows, channels), bf16),
        pltpu.VMEM((2, modes, channels), f32),
        pltpu.VMEM(table.shape, bf16),
        pltpu.VMEM((4, rows, channels), bf16),
        pltpu.VMEM((2, 1, channels), f32),
        pltpu.VMEM(w1.shape, bf16),
        pltpu.VMEM(w2.shape, bf16),
        pltpu.VMEM((pieces, 2 * rows, NARROW), bf16),
        pltpu.VMEM((pieces, 2 * rows, NARROW), f32),
        pltpu.VMEM((chunks, 2 * rows, WIDE), f32),
        pltpu.VMEM((NODES, modes, channels), f32),
        pltpu.VMEM((modes, NODES, channels), f32),
        pltpu.VMEM((NODES, channels), f32),
        pltpu.VMEM((modes, channels), f32),
        pltpu.VMEM((modes, channels), f32),
        pltpu.VMEM((modes, channels), f32),
        pltpu.VMEM((rows, channels), f32),
        pltpu.VMEM((chunks, rows, WIDE), f32),
        pltpu.VMEM((chunks, rows, WIDE), bf16),
        pltpu.VMEM((OWNERS, tiles * modes, LANES), bf16),
        pltpu.VMEM((OWNERS, tiles * modes, LANES), bf16),
        pltpu.VMEM((OWNERS, tiles * modes, LANES), bf16),
        pltpu.VMEM((n // 2, tiles * modes, LANES), bf16),
        pltpu.VMEM((n // 2, tiles * modes, LANES), bf16),
        pltpu.VMEM((OWNERS, tiles * modes, LANES), bf16),
        pltpu.SemaphoreType.DMA((7,)),
        pltpu.SemaphoreType.DMA((chunks + 2,)),
        pltpu.SemaphoreType.DMA((n // minor,)),
        pltpu.SemaphoreType.DMA((1,)),
        pltpu.SemaphoreType.DMA((1,)),
        pltpu.SemaphoreType.DMA((1,)),
        pltpu.SemaphoreType.REGULAR,
    ]
    mixed = pl.pallas_call(
        functools.partial(kernel, n, minor, nodes),
        out_shape=pltpu.VMEM((rows, channels), bf16),
        in_specs=[pl.BlockSpec(memory_space=pltpu.HBM)] * len(operands),
        out_specs=pl.BlockSpec(memory_space=pltpu.VMEM),
        scratch_shapes=scratch,
        compiler_params=pltpu.CompilerParams(
            collective_id=0, has_side_effects=True, vmem_limit_bytes=56 * 1024 * 1024
        ),
    )(*operands)
    return pl.pallas_call(
        store,
        out_shape=jax.ShapeDtypeStruct((rows, channels), bf16),
        in_specs=[pl.BlockSpec(memory_space=pl.ANY)],
        out_specs=pl.BlockSpec(memory_space=pl.ANY),
        scratch_shapes=[pltpu.SemaphoreType.DMA((1,))],
    )(pltpu.with_memory_space_constraint(mixed, pltpu.VMEM))


def solution(mesh):
    s, r = P(axes, None), P()
    specs = (s, s, s, r, r, r, s, s, r, r, r, r)
    return jax.shard_map(local, mesh=mesh, in_specs=specs, out_specs=s, check_vma=False)
```
